512 devices in a mesh: group: 16 (over x_hi, y), shard: 32 (over x_lo, z, core).
Axes of the slice: x: 4 (x_hi: 2, x_lo: 2; x = x_hi * 2 + x_lo), y: 8, z: 8, core: 2. Of those that a mesh axis runs over, the one named last changes fastest.
Arguments:
- factors: bfloat16 [128, 6144, 1024], P('group', 'shard'), may hold values from -0.15625 to 0.15625
- amplitudes: bfloat16 [64, 32, 1024], P('group'), may hold values from -6 to 6
- factor_route: int32 [16, 16], P('group'), may hold values from 0 to 7
- amp_route: int32 [16, 16], P('group'), may hold values from 0 to 3
- task_list: int32 [16, 3, 4], P('group'), may hold values from 0 to 15
- target_tile: int32 [16, 16], P('group'), may hold values from 0 to 1
Outputs:
- residual: float32 [32, 32, 1024], P('group', None, 'shard')
The draws below stay inside these ranges and needn't reach their ends.
Inputs may be any that keep to these rules, and one draw needn't show every extreme that they name: task_list[h, k] names the group that owns the residual tile and the groups that send the two factor blocks and the amplitude tile used by task k of helper group h.
All inputs are finite; a program needn't handle non-finite values.
Results may differ from the reference program's by a relative error of at most 0.0025.
Values may be sent and summed in bfloat16 or wider, within the bound.
No kernel may reach another device: no remote copies, remote signals or barrier semaphores. Data moves between devices by JAX's collectives and lax.ppermute only.
A program may use at most 128 MiB of HBM per device.

```python
import jax
import jax.numpy as jnp
from jax import lax

VB = 32
NAUX = 6144
OCC = 32
TASKS = 3
FPG = 8
APG = 4
TPG = 2
TW = 1024
NF = 128
NA = 64
N_GROUP = 16
N_SHARD = 32


def plant(values, own_key, least, largest):
    place = [jax.random.randint(jax.random.fold_in(own_key, axis), (), 0, length) for axis, length in enumerate(values.shape)]
    main_axis = values.shape.index(max(values.shape))
    neighbour = place[:main_axis] + [(place[main_axis] + 1) % values.shape[main_axis]] + place[main_axis + 1:]
    return values.at[tuple(place)].set(least).at[tuple(neighbour)].set(largest)


def spiked(values, stream_key, source, target, shards_of, factor):
    def block_of(dim):
        return (jnp.arange(values.shape[dim]) // (values.shape[dim] // shards_of)).reshape((-1,) + (1,) * (values.ndim - 1 - dim))

    near = jax.random.permutation(stream_key, shards_of)[block_of(target)]
    other_side = (block_of(target) + shards_of // 2) % shards_of
    return jnp.where((block_of(source) == near) | (block_of(source) == other_side), factor * values, values)


def shard_levels(own_key, shape, cuts, smallest, high):
    loudness = 1.0
    for position, blocks in cuts:
        steps = jax.random.uniform(jax.random.fold_in(jax.random.fold_in(own_key, 6), position), (blocks,), jnp.float32, smallest / len(cuts), high / len(cuts))
        loudness = loudness * jnp.repeat(jnp.exp(steps), shape[position] // blocks).reshape((-1,) + (1,) * (len(shape) - 1 - position))
    return loudness


def scatter_about(stream_key, dims, width, limit, shards=(), kind=jnp.bfloat16):
    values = jax.random.normal(stream_key, dims, jnp.float32) * width
    if len(shards) > 0:
        values = shard_levels(stream_key, dims, shards, -0.22, 0.18) * values
    return jnp.clip(values, min=-limit, max=limit).astype(kind)


def bell_draw_with(key, shape, scale, bound, cuts, heavy, kind=jnp.bfloat16):
    values = scale * jax.random.normal(key, shape, jnp.float32)
    if cuts:
        values = values * shard_levels(key, shape, cuts, -0.22, 0.18)
    return jnp.clip(spiked(values, jax.random.fold_in(key, 3), *heavy), -bound, bound).astype(kind)


def setup_inputs(seed: int = 0) -> dict:
    arg_keys = jax.random.split(jax.random.key(seed), 7)
    return {
        "factors": bell_draw_with(arg_keys[0], (NF, NAUX, TW), NAUX ** -0.5, 0.15625, ((0, 16), (1, 32)), (1, 2, 32, 2.75)),
        "amplitudes": scatter_about(arg_keys[1], (NA, OCC, TW), 1.0, 6.0, ((0, 16),)),
        "factor_route": plant(jax.random.randint(arg_keys[2], (N_GROUP, N_GROUP), 0, FPG), jax.random.fold_in(arg_keys[2], 1), 0, FPG - 1).astype(jnp.int32),
        "amp_route": plant(jax.random.randint(arg_keys[3], (N_GROUP, N_GROUP), 0, APG), jax.random.fold_in(arg_keys[3], 1), 0, APG - 1).astype(jnp.int32),
        "task_list": plant(jax.random.randint(arg_keys[4], (N_GROUP, TASKS, 4), 0, N_GROUP), jax.random.fold_in(arg_keys[4], 1), 0, N_GROUP - 1).astype(jnp.int32),
        "target_tile": plant(jax.random.randint(arg_keys[5], (N_GROUP, N_GROUP), 0, TPG), jax.random.fold_in(arg_keys[5], 1), 0, TPG - 1).astype(jnp.int32),
    }


def shard_terms(left_block, right_block, amplitude):
    quota = NAUX // N_SHARD
    left_parts = left_block.reshape(N_SHARD, quota, VB * VB)
    right_parts = right_block.reshape(N_SHARD, quota, VB * VB)

    def add_shard(total, pieces):
        left_piece, right_piece = pieces
        products = jnp.dot(left_piece.T, right_piece, preferred_element_type=jnp.float32)
        integral = products.reshape(VB, VB, VB, VB).transpose(0, 2, 1, 3).reshape(VB * VB, VB * VB)
        integral = integral.astype(jnp.bfloat16)
        return total + jnp.dot(amplitude, integral.T, preferred_element_type=jnp.float32), None

    start = jnp.zeros((OCC, VB * VB), jnp.float32)
    total, unused = lax.scan(add_shard, start, (left_parts, right_parts))
    return total


def reference(factors, amplitudes, factor_route, amp_route, task_list, target_tile):
    helper_ids = jnp.repeat(jnp.arange(N_GROUP, dtype=jnp.int32), TASKS)
    task_ids = jnp.tile(jnp.arange(TASKS, dtype=jnp.int32), N_GROUP)

    def ladder_task(result, entries):
        helper, task_index = entries
        record = task_list[helper, task_index]
        owner = record[0]
        first_src = record[1]
        second_src = record[2]
        amp_src = record[3]
        left_block = factors[(first_src * FPG + factor_route[first_src, helper]).astype(jnp.int32)]
        right_block = factors[(second_src * FPG + factor_route[second_src, helper]).astype(jnp.int32)]
        amplitude = amplitudes[(amp_src * APG + amp_route[amp_src, helper]).astype(jnp.int32)]
        tile_index = (owner * TPG + target_tile[owner, helper]).astype(jnp.int32)
        contribution = shard_terms(left_block, right_block, amplitude)
        return result.at[tile_index].add(contribution), None

    result = jnp.zeros((TPG * N_GROUP, OCC, VB * VB), jnp.float32)
    result, unused = lax.scan(ladder_task, result, (helper_ids, task_ids))
    return result
```

```python
import functools

import jax
import jax.numpy as jnp
from jax import lax
from jax.experimental import pallas as pl
from jax.experimental.pallas import tpu as pltpu
from jax.sharding import PartitionSpec as P

VB = 32
TPG = 2
LANES = 128
FOLD = LANES // VB


def swap_lane_blocks(tiles):
    lane = lax.broadcasted_iota(jnp.int32, tiles[0].shape, 1)
    x0, x1, x2, x3 = tiles
    low = lane < 2 * VB
    y0 = jnp.where(low, x0, pltpu.roll(x2, 2 * VB, 1))
    y2 = jnp.where(low, pltpu.roll(x0, 2 * VB, 1), x2)
    y1 = jnp.where(low, x1, pltpu.roll(x3, 2 * VB, 1))
    y3 = jnp.where(low, pltpu.roll(x1, 2 * VB, 1), x3)
    even = lane % (2 * VB) < VB
    z0 = jnp.where(even, y0, pltpu.roll(y1, VB, 1))
    z1 = jnp.where(even, pltpu.roll(y0, LANES - VB, 1), y1)
    z2 = jnp.where(even, y2, pltpu.roll(y3, VB, 1))
    z3 = jnp.where(even, pltpu.roll(y2, LANES - VB, 1), y3)
    return z0, z1, z2, z3


def ladder_kernel(record, left, right, amp, swap, out, folded, result):
    width = left.shape[2]
    occupied = amp.shape[1]
    per_pass = 2 * FOLD
    span = per_pass * VB
    right_t = jnp.dot(right[0], swap[...], preferred_element_type=jnp.float32).astype(jnp.bfloat16)
    amp_t = jnp.dot(amp[0], swap[...], preferred_element_type=jnp.float32).astype(jnp.bfloat16)
    for step in range(VB // per_pass):
        columns = slice(step * span, (step + 1) * span)
        integral = lax.dot_general(
            left[0, :, columns], right_t, (((0,), (0,)), ((), ())), preferred_element_type=jnp.float32
        )
        for half in range(2):
            for part in range(width // LANES):
                lanes = slice(part * LANES, (part + 1) * LANES)
                rows = half * FOLD * VB
                tiles = [integral[rows + a * VB : rows + (a + 1) * VB, lanes] for a in range(FOLD)]
                for d, tile in enumerate(swap_lane_blocks(tiles)):
                    base = (part * FOLD + d) * VB
                    folded[base : base + VB, half * LANES : (half + 1) * LANES] = tile.astype(jnp.bfloat16)
        result[:, columns] = jnp.dot(amp_t, folded[...], preferred_element_type=jnp.float32)
    band = occupied // FOLD
    for group in range(width // LANES):
        lanes = slice(group * LANES, (group + 1) * LANES)
        tiles = [result[i * band : (i + 1) * band, lanes] for i in range(FOLD)]
        for a, tile in enumerate(swap_lane_blocks(tiles)):
            out[group * FOLD + a, 0] = tile


def ladder(records, factors, amps):
    tasks = records.shape[0]
    rows, width = factors.shape[1:]
    occupied = amps.shape[1]
    index = jnp.arange(width, dtype=jnp.int32)
    swap = (
        (index[:, None] // VB == index[None, :] % VB) & (index[:, None] % VB == index[None, :] // VB)
    ).astype(jnp.bfloat16)
    band = occupied // FOLD
    return pl.pallas_call(
        ladder_kernel,
        grid_spec=pltpu.PrefetchScalarGridSpec(
            num_scalar_prefetch=1,
            grid=(tasks,),
            in_specs=[
                pl.BlockSpec((1, rows, width), lambda k, rec: (rec[k, 1], 0, 0)),
                pl.BlockSpec((1, rows, width), lambda k, rec: (rec[k, 2], 0, 0)),
                pl.BlockSpec((1, occupied, width), lambda k, rec: (rec[k, 3], 0, 0)),
                pl.BlockSpec((width, width), lambda k, rec: (0, 0)),
            ],
            out_specs=pl.BlockSpec((VB, 1, band, LANES), lambda k, rec: (0, k, 0, 0)),
            scratch_shapes=[
                pltpu.VMEM((width, 2 * LANES), jnp.bfloat16),
                pltpu.VMEM((occupied, width), jnp.float32),
            ],
        ),
        out_shape=jax.ShapeDtypeStruct((VB, tasks, band, LANES), jnp.float32),
        compiler_params=pltpu.CompilerParams(dimension_semantics=("arbitrary",)),
        name="ladder",
    )(records, factors, factors, amps, swap)


def combine_kernel(record, pieces, out):
    tasks = record.shape[0]
    total = jnp.sum(pieces[...], axis=0)
    out[...] = jnp.zeros_like(out)
    for k in range(tasks):
        owner = record[k, 0]
        out[owner] += total[k]


def combine(records, pieces, groups):
    return pl.pallas_call(
        combine_kernel,
        in_specs=[pl.BlockSpec(memory_space=pltpu.SMEM), pl.BlockSpec(memory_space=pltpu.VMEM)],
        out_specs=pl.BlockSpec(memory_space=pltpu.VMEM),
        out_shape=jax.ShapeDtypeStruct((groups, *pieces.shape[2:]), jnp.float32),
        name="combine",
    )(records, pieces)


def owned_kernel(tile, arrived, out, total):
    groups, band, lanes = arrived.shape
    total[...] = jnp.zeros_like(total)
    for h in range(groups):
        total[tile[h]] += arrived[h]
    for t in range(TPG):
        for i in range(FOLD):
            out[t, i * band : (i + 1) * band, :] = total[t][:, i * VB : (i + 1) * VB]


def owned(tile, arrived):
    groups, band, lanes = arrived.shape
    return pl.pallas_call(
        owned_kernel,
        in_specs=[pl.BlockSpec(memory_space=pltpu.SMEM), pl.BlockSpec(memory_space=pltpu.VMEM)],
        out_specs=pl.BlockSpec(memory_space=pltpu.VMEM),
        out_shape=jax.ShapeDtypeStruct((TPG, band * FOLD, VB), jnp.float32),
        scratch_shapes=[pltpu.VMEM((TPG, band, lanes), jnp.float32)],
        name="owned",
    )(tile, arrived)


def body(factors, amplitudes, factor_route, amp_route, task_list, target_tile):
    groups = lax.axis_size("group")
    records = task_list[0]
    factor_send = factors.at[factor_route[0]].get(mode="promise_in_bounds")
    amp_send = amplitudes.at[amp_route[0]].get(mode="promise_in_bounds")
    amp_recv = lax.all_to_all(amp_send, "group", split_axis=0, concat_axis=0, tiled=True)
    factor_recv = lax.all_to_all(factor_send, "group", split_axis=0, concat_axis=0, tiled=True)
    parts = ladder(records, factor_recv, amp_recv)
    pieces = lax.all_to_all(parts, "shard", split_axis=0, concat_axis=0, tiled=True)
    returns = combine(records, pieces, groups)
    arrived = lax.all_to_all(returns, "group", split_axis=0, concat_axis=0, tiled=True)
    return owned(target_tile[0], arrived)


def solution(mesh):
    return jax.shard_map(
        body,
        mesh=mesh,
        in_specs=(
            P("group", "shard", None),
            P("group", None, None),
            P("group", None),
            P("group", None),
            P("group", None, None),
            P("group", None),
        ),
        out_specs=P("group", None, "shard"),
        check_vma=False,
    )
```

```python
import functools

import jax
import jax.numpy as jnp
from jax import lax
from jax.experimental import pallas as pl
from jax.experimental.pallas import tpu as pltpu
from jax.sharding import PartitionSpec as P

VB = 32
TPG = 2
LANES = 128
FOLD = LANES // VB


def swap_lane_blocks(tiles):
    lane = lax.broadcasted_iota(jnp.int32, tiles[0].shape, 1)
    x0, x1, x2, x3 = tiles
    low = lane < 2 * VB
    y0 = jnp.where(low, x0, pltpu.roll(x2, 2 * VB, 1))
    y2 = jnp.where(low, pltpu.roll(x0, 2 * VB, 1), x2)
    y1 = jnp.where(low, x1, pltpu.roll(x3, 2 * VB, 1))
    y3 = jnp.where(low, pltpu.roll(x1, 2 * VB, 1), x3)
    even = lane % (2 * VB) < VB
    z0 = jnp.where(even, y0, pltpu.roll(y1, VB, 1))
    z1 = jnp.where(even, pltpu.roll(y0, LANES - VB, 1), y1)
    z2 = jnp.where(even, y2, pltpu.roll(y3, VB, 1))
    z3 = jnp.where(even, pltpu.roll(y2, LANES - VB, 1), y3)
    return z0, z1, z2, z3


def ladder_kernel(record, left, right, amp, swap, out, folded, result):
    width = left.shape[2]
    occupied = amp.shape[1]
    per_pass = 2 * FOLD
    span = per_pass * VB
    right_t = jnp.dot(right[0], swap[...], preferred_element_type=jnp.float32).astype(jnp.bfloat16)
    amp_t = jnp.dot(amp[0], swap[...], preferred_element_type=jnp.float32).astype(jnp.bfloat16)
    for step in range(VB // per_pass):
        columns = slice(step * span, (step + 1) * span)
        integral = lax.dot_general(
            left[0, :, columns], right_t, (((0,), (0,)), ((), ())), preferred_element_type=jnp.float32
        )
        for half in range(2):
            for part in range(width // LANES):
                lanes = slice(part * LANES, (part + 1) * LANES)
                rows = half * FOLD * VB
                tiles = [integral[rows + a * VB : rows + (a + 1) * VB, lanes] for a in range(FOLD)]
                for d, tile in enumerate(swap_lane_blocks(tiles)):
                    base = (part * FOLD + d) * VB
                    folded[base : base + VB, half * LANES : (half + 1) * LANES] = tile.astype(jnp.bfloat16)
        result[:, columns] = jnp.dot(amp_t, folded[...], preferred_element_type=jnp.float32)
    band = occupied // FOLD
    for group in range(width // LANES):
        lanes = slice(group * LANES, (group + 1) * LANES)
        tiles = [result[i * band : (i + 1) * band, lanes] for i in range(FOLD)]
        for a, tile in enumerate(swap_lane_blocks(tiles)):
            out[group * FOLD + a, 0] = tile


def ladder(records, factors, amps):
    tasks = records.shape[0]
    rows, width = factors.shape[1:]
    occupied = amps.shape[1]
    index = jnp.arange(width, dtype=jnp.int32)
    swap = (
        (index[:, None] // VB == index[None, :] % VB) & (index[:, None] % VB == index[None, :] // VB)
    ).astype(jnp.bfloat16)
    band = occupied // FOLD
    return pl.pallas_call(
        ladder_kernel,
        grid_spec=pltpu.PrefetchScalarGridSpec(
            num_scalar_prefetch=1,
            grid=(tasks,),
            in_specs=[
                pl.BlockSpec((1, rows, width), lambda k, rec: (rec[k, 1], 0, 0)),
                pl.BlockSpec((1, rows, width), lambda k, rec: (rec[k, 2], 0, 0)),
                pl.BlockSpec((1, occupied, width), lambda k, rec: (k, 0, 0)),
                pl.BlockSpec((width, width), lambda k, rec: (0, 0)),
            ],
            out_specs=pl.BlockSpec((VB, 1, band, LANES), lambda k, rec: (0, k, 0, 0)),
            scratch_shapes=[
                pltpu.VMEM((width, 2 * LANES), jnp.bfloat16),
                pltpu.VMEM((occupied, width), jnp.float32),
            ],
        ),
        out_shape=jax.ShapeDtypeStruct((VB, tasks, band, LANES), jnp.float32),
        compiler_params=pltpu.CompilerParams(dimension_semantics=("arbitrary",)),
        name="ladder",
    )(records, factors, factors, amps, swap)


def combine_kernel(record, pieces, out):
    tasks = record.shape[0]
    total = jnp.sum(pieces[...], axis=0)
    out[...] = jnp.zeros_like(out)
    for k in range(tasks):
        owner = record[k, 0]
        out[owner] += total[k]


def combine(records, pieces, groups):
    return pl.pallas_call(
        combine_kernel,
        in_specs=[pl.BlockSpec(memory_space=pltpu.SMEM), pl.BlockSpec(memory_space=pltpu.VMEM)],
        out_specs=pl.BlockSpec(memory_space=pltpu.VMEM),
        out_shape=jax.ShapeDtypeStruct((groups, *pieces.shape[2:]), jnp.float32),
        name="combine",
    )(records, pieces)


def owned_kernel(tile, arrived, out, total):
    groups, band, lanes = arrived.shape
    total[...] = jnp.zeros_like(total)
    for h in range(groups):
        total[tile[h]] += arrived[h]
    for t in range(TPG):
        for i in range(FOLD):
            out[t, i * band : (i + 1) * band, :] = total[t][:, i * VB : (i + 1) * VB]


def owned(tile, arrived):
    groups, band, lanes = arrived.shape
    return pl.pallas_call(
        owned_kernel,
        in_specs=[pl.BlockSpec(memory_space=pltpu.SMEM), pl.BlockSpec(memory_space=pltpu.VMEM)],
        out_specs=pl.BlockSpec(memory_space=pltpu.VMEM),
        out_shape=jax.ShapeDtypeStruct((TPG, band * FOLD, VB), jnp.float32),
        scratch_shapes=[pltpu.VMEM((TPG, band, lanes), jnp.float32)],
        name="owned",
    )(tile, arrived)


def spread(block, axis):
    members = lax.axis_size(axis)
    me = lax.axis_index(axis)
    held = block[None]
    bit = 1
    while bit < members:
        other = lax.ppermute(held, axis, [(i, i ^ bit) for i in range(members)])
        mine_first = (me & bit) == 0
        held = jnp.where(
            mine_first, jnp.concatenate([held, other]), jnp.concatenate([other, held])
        )
        bit *= 2
    return held


def amplitude_tiles(records, amplitudes, amp_route):
    group, shard = lax.axis_index("group"), lax.axis_index("shard")
    tiles, _, width = amplitudes.shape
    tasks = records.shape[0]
    rows = lax.dynamic_index_in_dim(amplitudes, shard, 1, keepdims=False)
    route = jnp.pad(amp_route[0], (0, width - amp_route.shape[1])).astype(rows.dtype)
    block = jnp.concatenate([rows, route[None], jnp.zeros((8 - tiles - 1, width), rows.dtype)])
    held = spread(block, "group")
    source = records[:, 3]
    routes = held[:, tiles, : amp_route.shape[1]].astype(jnp.int32)[:, group]
    picked = [
        lax.dynamic_slice(held, (source[k], routes[source[k]], 0), (1, 1, width))[0, 0] for k in range(tasks)
    ]
    whole = spread(jnp.stack(picked), "shard")
    return whole.transpose(1, 0, 2)


def body(factors, amplitudes, factor_route, amp_route, task_list, target_tile):
    groups = lax.axis_size("group")
    records = task_list[0]
    factor_send = factors.at[factor_route[0]].get(mode="promise_in_bounds")
    amps = amplitude_tiles(records, amplitudes, amp_route)
    factor_recv = lax.all_to_all(factor_send, "group", split_axis=0, concat_axis=0, tiled=True)
    parts = ladder(records, factor_recv, amps)
    pieces = lax.all_to_all(parts, "shard", split_axis=0, concat_axis=0, tiled=True)
    returns = combine(records, pieces, groups)
    arrived = lax.all_to_all(returns, "group", split_axis=0, concat_axis=0, tiled=True)
    return owned(target_tile[0], arrived)


def solution(mesh):
    return jax.shard_map(
        body,
        mesh=mesh,
        in_specs=(
            P("group", "shard", None),
            P("group", None, None),
            P("group", None),
            P("group", None),
            P("group", None, None),
            P("group", None),
        ),
        out_specs=P("group", None, "shard"),
        check_vma=False,
    )
```

```python
import functools

import jax
import jax.numpy as jnp
from jax import lax
from jax.experimental import pallas as pl
from jax.experimental.pallas import tpu as pltpu
from jax.sharding import PartitionSpec as P

VB = 32
TPG = 2
LANES = 128
FOLD = LANES // VB


def swap_lane_blocks(tiles):
    lane = lax.broadcasted_iota(jnp.int32, tiles[0].shape, 1)
    low = lane.astype(tiles[0].dtype) < 2 * VB
    even = (lane % (2 * VB)).astype(tiles[0].dtype) < VB
    x0, x1, x2, x3 = tiles
    y0 = jnp.where(low, x0, pltpu.roll(x2, 2 * VB, 1))
    y2 = jnp.where(low, pltpu.roll(x0, 2 * VB, 1), x2)
    y1 = jnp.where(low, x1, pltpu.roll(x3, 2 * VB, 1))
    y3 = jnp.where(low, pltpu.roll(x1, 2 * VB, 1), x3)
    z0 = jnp.where(even, y0, pltpu.roll(y1, VB, 1))
    z1 = jnp.where(even, pltpu.roll(y0, LANES - VB, 1), y1)
    z2 = jnp.where(even, y2, pltpu.roll(y3, VB, 1))
    z3 = jnp.where(even, pltpu.roll(y2, LANES - VB, 1), y3)
    return z0, z1, z2, z3


def ladder_kernel(record, left, right, amp, swap, out, right_t, amp_t, integral, folded, result):
    width = left.shape[2]
    occupied = amp.shape[1]
    per_pass = 2 * FOLD
    span = per_pass * VB
    right_t[...] = jnp.dot(right[0], swap[...], preferred_element_type=jnp.float32).astype(jnp.bfloat16)
    amp_t[...] = jnp.dot(amp[0], swap[...], preferred_element_type=jnp.float32).astype(jnp.bfloat16)

    def products(step, _):
        columns = pl.ds(pl.multiple_of(step * 2 * span, 2 * span), 2 * span)
        integral[columns, :] = lax.dot_general(
            left[0, :, columns], right_t[...], (((0,), (0,)), ((), ())), preferred_element_type=jnp.float32
        ).astype(jnp.bfloat16)
        return 0

    lax.fori_loop(0, VB // per_pass // 2, products, 0)

    def one_pass(step, _):
        columns = pl.ds(pl.multiple_of(step * span, span), span)
        for part in range(width // LANES):
            lanes = slice(part * LANES, (part + 1) * LANES)
            for half in range(2):
                rows = half * FOLD * VB
                tiles = [
                    integral[pl.ds(pl.multiple_of(step * span + rows + a * VB, VB), VB), lanes] for a in range(FOLD)
                ]
                for d, tile in enumerate(swap_lane_blocks(tiles)):
                    base = (part * FOLD + d) * VB
                    folded[base : base + VB, half * LANES : (half + 1) * LANES] = tile
        result[:, columns] = jnp.dot(amp_t[...], folded[...], preferred_element_type=jnp.float32)
        return 0

    lax.fori_loop(0, VB // per_pass, one_pass, 0)
    band = occupied // FOLD
    for group in range(width // LANES):
        lanes = slice(group * LANES, (group + 1) * LANES)
        tiles = [result[i * band : (i + 1) * band, lanes] for i in range(FOLD)]
        for a, tile in enumerate(swap_lane_blocks(tiles)):
            out[group * FOLD + a, 0] = tile


def ladder(records, factors, amps):
    tasks = records.shape[0]
    rows, width = factors.shape[1:]
    occupied = amps.shape[1]
    index = jnp.arange(width, dtype=jnp.int32)
    swap = (
        (index[:, None] // VB == index[None, :] % VB) & (index[:, None] % VB == index[None, :] // VB)
    ).astype(jnp.bfloat16)
    band = occupied // FOLD
    return pl.pallas_call(
        ladder_kernel,
        grid_spec=pltpu.PrefetchScalarGridSpec(
            num_scalar_prefetch=1,
            grid=(tasks,),
            in_specs=[
                pl.BlockSpec((1, rows, width), lambda k, rec: (rec[k, 1], 0, 0)),
                pl.BlockSpec((1, rows, width), lambda k, rec: (rec[k, 2], 0, 0)),
                pl.BlockSpec((1, occupied, width), lambda k, rec: (k, 0, 0)),
                pl.BlockSpec((width, width), lambda k, rec: (0, 0)),
            ],
            out_specs=pl.BlockSpec((VB, 1, band, LANES), lambda k, rec: (0, k, 0, 0)),
            scratch_shapes=[
                pltpu.VMEM((rows, width), jnp.bfloat16),
                pltpu.VMEM((occupied, width), jnp.bfloat16),
                pltpu.VMEM((width, width), jnp.bfloat16),
                pltpu.VMEM((width, 2 * LANES), jnp.bfloat16),
                pltpu.VMEM((occupied, width), jnp.float32),
            ],
        ),
        out_shape=jax.ShapeDtypeStruct((VB, tasks, band, LANES), jnp.float32),
        compiler_params=pltpu.CompilerParams(dimension_semantics=("arbitrary",)),
        name="ladder",
    )(records, factors, factors, amps, swap)


def combine_kernel(record, pieces, out):
    tasks = record.shape[0]
    total = jnp.sum(pieces[...], axis=0)
    out[...] = jnp.zeros_like(out)
    for k in range(tasks):
        owner = record[k, 0]
        out[owner] += total[k]


def combine(records, pieces, groups):
    return pl.pallas_call(
        combine_kernel,
        in_specs=[pl.BlockSpec(memory_space=pltpu.SMEM), pl.BlockSpec(memory_space=pltpu.VMEM)],
        out_specs=pl.BlockSpec(memory_space=pltpu.VMEM),
        out_shape=jax.ShapeDtypeStruct((groups, *pieces.shape[2:]), jnp.float32),
        name="combine",
    )(records, pieces)


def owned_kernel(tile, arrived, out, total):
    groups, band, lanes = arrived.shape
    total[...] = jnp.zeros_like(total)
    for h in range(groups):
        total[tile[h]] += arrived[h]
    for t in range(TPG):
        for i in range(FOLD):
            out[t, i * band : (i + 1) * band, :] = total[t][:, i * VB : (i + 1) * VB]


def owned(tile, arrived):
    groups, band, lanes = arrived.shape
    return pl.pallas_call(
        owned_kernel,
        in_specs=[pl.BlockSpec(memory_space=pltpu.SMEM), pl.BlockSpec(memory_space=pltpu.VMEM)],
        out_specs=pl.BlockSpec(memory_space=pltpu.VMEM),
        out_shape=jax.ShapeDtypeStruct((TPG, band * FOLD, VB), jnp.float32),
        scratch_shapes=[pltpu.VMEM((TPG, band, lanes), jnp.float32)],
        name="owned",
    )(tile, arrived)


def spread(block, axis):
    members = lax.axis_size(axis)
    me = lax.axis_index(axis)
    held = block[None]
    bit = 1
    while bit < members:
        other = lax.ppermute(held, axis, [(i, i ^ bit) for i in range(members)])
        mine_first = (me & bit) == 0
        held = jnp.where(
            mine_first, jnp.concatenate([held, other]), jnp.concatenate([other, held])
        )
        bit *= 2
    return held


def amplitude_tiles(records, amplitudes, amp_route):
    shard = lax.axis_index("shard")
    width = amplitudes.shape[2]
    rows = lax.dynamic_index_in_dim(amplitudes, shard, 1, keepdims=False)
    send = rows.at[amp_route[0]].get(mode="promise_in_bounds").reshape(-1, width // LANES, LANES)
    arrived = lax.all_to_all(send, "group", split_axis=0, concat_axis=0, tiled=True)
    return arrived.at[records[:, 3]].get(mode="promise_in_bounds")


def body(factors, amplitudes, factor_route, amp_route, task_list, target_tile):
    groups = lax.axis_size("group")
    records = task_list[0]
    factor_send = factors.at[factor_route[0]].get(mode="promise_in_bounds")
    picked = amplitude_tiles(records, amplitudes, amp_route)
    factor_send, picked = lax.optimization_barrier((factor_send, picked))
    factor_recv = lax.all_to_all(factor_send, "group", split_axis=0, concat_axis=0, tiled=True)
    amps = spread(picked, "shard").reshape(-1, records.shape[0], factors.shape[2]).transpose(1, 0, 2)
    parts = ladder(records, factor_recv, amps)
    pieces = lax.all_to_all(parts, "shard", split_axis=0, concat_axis=0, tiled=True)
    returns = combine(records, pieces, groups)
    arrived = lax.all_to_all(returns, "group", split_axis=0, concat_axis=0, tiled=True)
    return owned(target_tile[0], arrived)


def solution(mesh):
    return jax.shard_map(
        body,
        mesh=mesh,
        in_specs=(
            P("group", "shard", None),
            P("group", None, None),
            P("group", None),
            P("group", None),
            P("group", None, None),
            P("group", None),
        ),
        out_specs=P("group", None, "shard"),
        check_vma=False,
    )
```

```python
import functools

import jax
import jax.numpy as jnp
from jax import lax
from jax.experimental import pallas as pl
from jax.experimental.pallas import tpu as pltpu
from jax.sharding import PartitionSpec as P

VB = 32
FPG = 8
APG = 4
TPG = 2
TASKS = 3
LANES = 128
FAST = 4
SWEEPS = 12
FACTOR_ROUTE, TARGET, RECORDS = 16, 32, 48
FOLD = LANES // VB


def swap_lane_blocks(tiles):
    lane = lax.broadcasted_iota(jnp.int32, tiles[0].shape, 1)
    low = lane.astype(tiles[0].dtype) < 2 * VB
    even = (lane % (2 * VB)).astype(tiles[0].dtype) < VB
    x0, x1, x2, x3 = tiles
    y0 = jnp.where(low, x0, pltpu.roll(x2, 2 * VB, 1))
    y2 = jnp.where(low, pltpu.roll(x0, 2 * VB, 1), x2)
    y1 = jnp.where(low, x1, pltpu.roll(x3, 2 * VB, 1))
    y3 = jnp.where(low, pltpu.roll(x1, 2 * VB, 1), x3)
    z0 = jnp.where(even, y0, pltpu.roll(y1, VB, 1))
    z1 = jnp.where(even, pltpu.roll(y0, LANES - VB, 1), y1)
    z2 = jnp.where(even, y2, pltpu.roll(y3, VB, 1))
    z3 = jnp.where(even, pltpu.roll(y2, LANES - VB, 1), y3)
    return z0, z1, z2, z3


def assemble(select, whole, cut, out):
    @pl.when(select < FPG)
    def _():
        out[...] = whole[0]

    @pl.when(select >= FPG)
    def _():
        rows = cut.shape[2]
        for piece in range(cut.shape[0]):
            half, part = divmod(piece, out.shape[1] // LANES)
            out[half * rows : (half + 1) * rows, part * LANES : (part + 1) * LANES] = cut[piece, 0]


def ladder_kernel(
    plan, left_whole, left_cut, right_whole, right_cut, amp, swap, out,
    left, right, right_t, amp_t, integral, folded, result,
):
    task = pl.program_id(0)

    @pl.when(plan[task, 3] < 0)
    def _():
        out[...] = jnp.zeros_like(out)

    @pl.when(plan[task, 3] >= 0)
    def _():
        assemble(plan[task, 0], left_whole, left_cut, left)
        assemble(plan[task, 1], right_whole, right_cut, right)
        ladder_task(left, right, amp, swap, out, right_t, amp_t, integral, folded, result)


def ladder_task(left, right, amp, swap, out, right_t, amp_t, integral, folded, result):
    width = left.shape[1]
    occupied = amp.shape[1]
    per_pass = 2 * FOLD
    span = per_pass * VB
    right_t[...] = jnp.dot(right[...], swap[...], preferred_element_type=jnp.float32).astype(jnp.bfloat16)
    amp_t[...] = jnp.dot(amp[0], swap[...], preferred_element_type=jnp.float32).astype(jnp.bfloat16)

    def products(step, _):
        columns = pl.ds(pl.multiple_of(step * 2 * span, 2 * span), 2 * span)
        integral[columns, :] = lax.dot_general(
            left[:, columns], right_t[...], (((0,), (0,)), ((), ())), preferred_element_type=jnp.float32
        ).astype(jnp.bfloat16)
        return 0

    lax.fori_loop(0, VB // per_pass // 2, products, 0)

    def one_pass(step, _):
        columns = pl.ds(pl.multiple_of(step * span, span), span)
        for part in range(width // LANES):
            lanes = slice(part * LANES, (part + 1) * LANES)
            for half in range(2):
                rows = half * FOLD * VB
                tiles = [
                    integral[pl.ds(pl.multiple_of(step * span + rows + a * VB, VB), VB), lanes] for a in range(FOLD)
                ]
                for d, tile in enumerate(swap_lane_blocks(tiles)):
                    base = (part * FOLD + d) * VB
                    folded[base : base + VB, half * LANES : (half + 1) * LANES] = tile
        result[:, columns] = jnp.dot(amp_t[...], folded[...], preferred_element_type=jnp.float32)
        return 0

    lax.fori_loop(0, VB // per_pass, one_pass, 0)
    band = occupied // FOLD
    for group in range(width // LANES):
        lanes = slice(group * LANES, (group + 1) * LANES)
        tiles = [result[i * band : (i + 1) * band, lanes] for i in range(FOLD)]
        for a, tile in enumerate(swap_lane_blocks(tiles)):
            out[group * FOLD + a, 0] = tile


def ladder(plan, factors, arrived, amps):
    rows, width = factors.shape[1:]
    tasks, occupied = amps.shape[:2]
    index = jnp.arange(width, dtype=jnp.int32)
    swap = (
        (index[:, None] // VB == index[None, :] % VB) & (index[:, None] % VB == index[None, :] // VB)
    ).astype(jnp.bfloat16)
    band = occupied // FOLD
    pieces, _, piece_rows, _ = arrived.shape

    def whole(side):
        def place(k, plan):
            return jnp.where(plan[k, side] < FPG, plan[k, side], 0), 0, 0

        return pl.BlockSpec((1, rows, width), place)

    def cut(side):
        def place(k, plan):
            return 0, jnp.where(plan[k, side] < FPG, 0, plan[k, side] - FPG), 0, 0

        return pl.BlockSpec((pieces, 1, piece_rows, LANES), place)

    return pl.pallas_call(
        ladder_kernel,
        grid_spec=pltpu.PrefetchScalarGridSpec(
            num_scalar_prefetch=1,
            grid=(tasks,),
            in_specs=[
                whole(0),
                cut(0),
                whole(1),
                cut(1),
                pl.BlockSpec((1, occupied, width), lambda k, plan: (k, 0, 0)),
                pl.BlockSpec((width, width), lambda k, plan: (0, 0)),
            ],
            out_specs=pl.BlockSpec((VB, 1, band, LANES), lambda k, plan: (0, k, 0, 0)),
            scratch_shapes=[
                pltpu.VMEM((rows, width), jnp.bfloat16),
                pltpu.VMEM((rows, width), jnp.bfloat16),
                pltpu.VMEM((rows, width), jnp.bfloat16),
                pltpu.VMEM((occupied, width), jnp.bfloat16),
                pltpu.VMEM((width, width), jnp.bfloat16),
                pltpu.VMEM((width, 2 * LANES), jnp.bfloat16),
                pltpu.VMEM((occupied, width), jnp.float32),
            ],
        ),
        out_shape=jax.ShapeDtypeStruct((VB, tasks, band, LANES), jnp.float32),
        compiler_params=pltpu.CompilerParams(dimension_semantics=("arbitrary",)),
        name="ladder",
    )(plan, factors, arrived, factors, arrived, amps, swap)


def combine_kernel(plan, pieces, out):
    total = jnp.sum(pieces[...], axis=0)
    out[...] = jnp.zeros_like(out)
    for k in range(pieces.shape[1]):
        target = plan[k, 3]

        @pl.when(target >= 0)
        def _():
            out[target] += total[k]


def combine(plan, pieces, tiles):
    return pl.pallas_call(
        combine_kernel,
        in_specs=[pl.BlockSpec(memory_space=pltpu.SMEM), pl.BlockSpec(memory_space=pltpu.VMEM)],
        out_specs=pl.BlockSpec(memory_space=pltpu.VMEM),
        out_shape=jax.ShapeDtypeStruct((tiles, *pieces.shape[2:]), jnp.float32),
        name="combine",
    )(plan, pieces)


def owned_kernel(arrived, out):
    groups, tiles, band, lanes = arrived.shape
    for t in range(tiles):
        total = jnp.sum(arrived[:, t], axis=0)
        for i in range(FOLD):
            out[t, i * band : (i + 1) * band, :] = total[:, i * VB : (i + 1) * VB]


def owned(arrived):
    groups, tiles, band, lanes = arrived.shape
    return pl.pallas_call(
        owned_kernel,
        in_specs=[pl.BlockSpec(memory_space=pltpu.VMEM)],
        out_specs=pl.BlockSpec(memory_space=pltpu.VMEM),
        out_shape=jax.ShapeDtypeStruct((tiles, band * FOLD, VB), jnp.float32),
        name="owned",
    )(arrived)


def assign_kernel(
    me, table, send, pick, plan, balanced,
    compute, other, compute_block, other_block, load, sent, uses, filled, slots, where_sent,
):
    groups = table.shape[0]
    mine = me[0]
    for g in range(groups):
        load[g] = 0
        sent[g] = 0
        filled[g] = 0
        slots[g] = 0

    def clear(i, _):
        uses[i] = 0
        where_sent[i] = -1
        pick[i] = 0
        return 0

    lax.fori_loop(0, groups * FPG, clear, 0)
    for i in range(send.shape[0]):
        send[i] = 0
    for k in range(plan.shape[0]):
        for j in range(3):
            plan[k, j] = 0
        plan[k, 3] = -1

    def first_choice(h, _):
        for k in range(TASKS):
            s1, s2 = table[h, RECORDS + 4 * k + 1], table[h, RECORDS + 4 * k + 2]
            b1, b2 = table[s1, FACTOR_ROUTE + h], table[s2, FACTOR_ROUTE + h]
            n1, n2 = uses[s1 * FPG + b1], uses[s2 * FPG + b2]
            at_first = 2 * load[s1] - jnp.where(n2 > 0, 0, FAST - sent[s2])
            at_second = 2 * load[s2] - jnp.where(n1 > 0, 0, FAST - sent[s1])
            second = at_first > at_second
            c, o = jnp.where(second, s2, s1), jnp.where(second, s1, s2)
            y, x = jnp.where(second, b2, b1), jnp.where(second, b1, b2)
            n = jnp.where(second, n1, n2)
            moved = jnp.where(c != o, 1, 0)
            i = h * TASKS + k
            compute[i], other[i], compute_block[i], other_block[i] = c, o, y, x
            load[c] += 1
            sent[o] += jnp.where(n == 0, moved, 0)
            uses[o * FPG + x] = n + moved
        return 0

    lax.fori_loop(0, groups, first_choice, 0)
    over = lambda n: jnp.maximum(n - FAST, 0)

    def excess():
        total = 0
        for g in range(groups):
            total += over(load[g]) + over(sent[g])
        return total

    def sweep(state):
        def visit(i, bad):
            c, o = compute[i], other[i]
            wanted = (c != o) & ((load[c] > FAST) | (sent[o] > FAST))

            def flip(bad):
                y, x = compute_block[i], other_block[i]
                nc, no = uses[c * FPG + y], uses[o * FPG + x]
                less, more = jnp.where(no == 1, 1, 0), jnp.where(nc == 0, 1, 0)
                lc, lo, sc, so = load[c], load[o], sent[c], sent[o]
                change = over(lc - 1) - over(lc) + over(lo + 1) - over(lo)
                change += over(sc + more) - over(sc) + over(so - less) - over(so)

                def take(bad):
                    compute[i], other[i], compute_block[i], other_block[i] = o, c, x, y
                    load[c], load[o] = lc - 1, lo + 1
                    sent[c], sent[o] = sc + more, so - less
                    uses[c * FPG + y], uses[o * FPG + x] = nc + 1, no - 1
                    return bad + change

                return lax.cond(change <= 0, take, lambda bad: bad, bad)

            return lax.cond(wanted, flip, lambda bad: bad, bad)

        return state[0] + 1, lax.fori_loop(0, groups * TASKS, visit, state[1])

    _, bad = lax.while_loop(lambda s: (s[0] < SWEEPS) & (s[1] > 0), sweep, (jnp.int32(0), excess()))
    good = bad == 0
    balanced[0] = jnp.where(good, 1, 0)
    stride = jnp.where(good, FAST, FPG)

    def fetch(source, block, c):
        remote = source != c
        known = where_sent[source * FPG + block]
        fresh = remote & (known < 0)
        count = filled[source]
        at = jnp.where(fresh, count, known)
        filled[source] = count + jnp.where(fresh, 1, 0)
        where_sent[source * FPG + block] = at
        send[jnp.where(fresh & (source == mine), at, FPG)] = block
        slot = slots[c]
        slots[c] = slot + jnp.where(remote, 1, 0)
        pick[jnp.where(remote, c * FPG + slot, groups * FPG)] = source * stride + at
        return jnp.where(remote, FPG + slot, block)

    def deal(h, _):
        for k in range(TASKS):
            o, s1, s2, s3 = [table[h, RECORDS + 4 * k + j] for j in range(4)]
            c = jnp.where(good, compute[h * TASKS + k], h)
            left = fetch(s1, table[s1, FACTOR_ROUTE + h], c)
            right = fetch(s2, table[s2, FACTOR_ROUTE + h], c)
            t = load[c]
            load[c] = t + 1
            row = jnp.where(c == mine, t, FAST)
            plan[row, 0] = left
            plan[row, 1] = right
            plan[row, 2] = s3 * APG + table[s3, h]
            plan[row, 3] = o * TPG + table[o, TARGET + h]
        return 0

    for g in range(groups):
        load[g] = 0
    lax.fori_loop(0, groups, deal, 0)


def assign(me, table):
    groups = table.shape[0]
    smem = pl.BlockSpec(memory_space=pltpu.SMEM)
    one = lambda n: pltpu.SMEM((n,), jnp.int32)
    tasks = groups * TASKS
    return pl.pallas_call(
        assign_kernel,
        in_specs=[smem, smem],
        out_specs=[smem] * 4,
        out_shape=[
            jax.ShapeDtypeStruct((2 * FPG,), jnp.int32),
            jax.ShapeDtypeStruct(((groups + 1) * FPG,), jnp.int32),
            jax.ShapeDtypeStruct((2 * FAST, 4), jnp.int32),
            jax.ShapeDtypeStruct((1,), jnp.int32),
        ],
        scratch_shapes=[one(tasks)] * 4 + [one(groups)] * 2 + [one(groups * FPG)] + [one(groups)] * 2 + [one(groups * FPG)],
        name="assign",
    )(me, table)


def cut_kernel(send, block, out):
    rows = out.shape[2]
    for piece in range(out.shape[0]):
        half, part = divmod(piece, block.shape[2] // LANES)
        out[piece, 0] = block[0, half * rows : (half + 1) * rows, part * LANES : (part + 1) * LANES]


def cut_blocks(send, factors, count, pieces):
    _, rows, width = factors.shape
    piece_rows = rows * width // LANES // pieces
    return pl.pallas_call(
        cut_kernel,
        grid_spec=pltpu.PrefetchScalarGridSpec(
            num_scalar_prefetch=1,
            grid=(count,),
            in_specs=[pl.BlockSpec((1, rows, width), lambda i, send: (send[i], 0, 0))],
            out_specs=pl.BlockSpec((pieces, 1, piece_rows, LANES), lambda i, send: (0, i, 0, 0)),
        ),
        out_shape=jax.ShapeDtypeStruct((pieces, count, piece_rows, LANES), factors.dtype),
        compiler_params=pltpu.CompilerParams(dimension_semantics=("arbitrary",)),
        name="cut_blocks",
    )(send, factors)


def spread(block, axis):
    members = lax.axis_size(axis)
    me = lax.axis_index(axis)
    held = block[None]
    bit = 1
    while bit < members:
        other = lax.ppermute(held, axis, [(i, i ^ bit) for i in range(members)])
        mine_first = (me & bit) == 0
        held = jnp.where(
            mine_first, jnp.concatenate([held, other]), jnp.concatenate([other, held])
        )
        bit *= 2
    return held


def group_blocks(amplitudes, factor_route, amp_route, task_list, target_tile):
    groups = lax.axis_size("group")
    tiles, _, width = amplitudes.shape
    rows = lax.dynamic_index_in_dim(amplitudes, lax.axis_index("shard"), 1, keepdims=False)
    facts = jnp.concatenate([amp_route[0], factor_route[0], target_tile[0], task_list[0].reshape(-1)])
    facts = jnp.pad(facts, (0, width - facts.shape[0])).astype(rows.dtype)
    block = jnp.concatenate([rows, facts[None], jnp.zeros((8 - tiles - 1, width), rows.dtype)])
    held = lax.all_to_all(
        jnp.broadcast_to(block[None], (groups, *block.shape)), "group", split_axis=0, concat_axis=0, tiled=True
    )
    return held[:, :tiles].reshape(groups * tiles, width), held[:, tiles, :LANES].astype(jnp.int32)


def contributions(blocks_sent, slots, factors, amp_rows, send, pick, plan):
    groups = lax.axis_size("group")
    width = factors.shape[2]
    cut = cut_blocks(send, factors, blocks_sent, groups)
    held = lax.all_to_all(cut, "group", split_axis=0, concat_axis=0, tiled=True)
    chosen = amp_rows.at[plan[:FAST, 2]].get(mode="promise_in_bounds")
    amps = spread(chosen.reshape(FAST, width // LANES, LANES), "shard")
    amps = amps.reshape(-1, FAST, width).transpose(1, 0, 2)
    wanted = pick[: groups * FPG].reshape(groups, FPG)[:, :slots].reshape(-1)
    dealt = held.reshape(groups * blocks_sent, *held.shape[2:]).at[wanted].get(mode="promise_in_bounds")
    dealt = dealt.reshape(groups, slots, *held.shape[2:])
    arrived = lax.all_to_all(dealt, "group", split_axis=0, concat_axis=0, tiled=True)
    return ladder(plan, factors, arrived, amps)


def body(factors, amplitudes, factor_route, amp_route, task_list, target_tile):
    groups = lax.axis_size("group")
    amp_rows, table = group_blocks(amplitudes, factor_route, amp_route, task_list, target_tile)
    me = lax.axis_index("group").astype(jnp.int32).reshape(1)
    send, pick, plan, balanced = assign(me, table)
    operands = (factors, amp_rows, send, pick, plan)
    parts = lax.cond(
        balanced[0] == 1,
        functools.partial(contributions, FAST, FAST),
        functools.partial(contributions, FPG, 2 * TASKS),
        *operands,
    )
    pieces = lax.all_to_all(parts, "shard", split_axis=0, concat_axis=0, tiled=True)
    returns = combine(plan, pieces, groups * TPG)
    arrived = lax.all_to_all(returns, "group", split_axis=0, concat_axis=0, tiled=True)
    return owned(arrived.reshape(groups, TPG, *arrived.shape[1:]))


def solution(mesh):
    return jax.shard_map(
        body,
        mesh=mesh,
        in_specs=(
            P("group", "shard", None),
            P("group", None, None),
            P("group", None),
            P("group", None),
            P("group", None, None),
            P("group", None),
        ),
        out_specs=P("group", None, "shard"),
        check_vma=False,
    )
```

```python
import functools

import jax
import jax.numpy as jnp
from jax import lax
from jax.experimental import pallas as pl
from jax.experimental.pallas import tpu as pltpu
from jax.sharding import PartitionSpec as P

VB = 32
FPG = 8
APG = 4
TPG = 2
TASKS = 3
LANES = 128
FAST = 4
SWEEPS = 12
FACTOR_ROUTE, TARGET, RECORDS = 16, 32, 48
FOLD = LANES // VB


def swap_lane_blocks(tiles):
    lane = lax.broadcasted_iota(jnp.int32, tiles[0].shape, 1)
    low = lane.astype(tiles[0].dtype) < 2 * VB
    even = (lane % (2 * VB)).astype(tiles[0].dtype) < VB
    x0, x1, x2, x3 = tiles
    y0 = jnp.where(low, x0, pltpu.roll(x2, 2 * VB, 1))
    y2 = jnp.where(low, pltpu.roll(x0, 2 * VB, 1), x2)
    y1 = jnp.where(low, x1, pltpu.roll(x3, 2 * VB, 1))
    y3 = jnp.where(low, pltpu.roll(x1, 2 * VB, 1), x3)
    z0 = jnp.where(even, y0, pltpu.roll(y1, VB, 1))
    z1 = jnp.where(even, pltpu.roll(y0, LANES - VB, 1), y1)
    z2 = jnp.where(even, y2, pltpu.roll(y3, VB, 1))
    z3 = jnp.where(even, pltpu.roll(y2, LANES - VB, 1), y3)
    return z0, z1, z2, z3


def assemble(select, whole, cut, out):
    @pl.when(select < FPG)
    def _():
        out[...] = whole[0]

    @pl.when(select >= FPG)
    def _():
        rows = cut.shape[2]
        for piece in range(cut.shape[0]):
            half, part = divmod(piece, out.shape[1] // LANES)
            out[half * rows : (half + 1) * rows, part * LANES : (part + 1) * LANES] = cut[piece, 0]


def ladder_kernel(
    plan, left_whole, left_cut, right_whole, right_cut, amp, swap, out,
    left, right, right_t, amp_t, integral, folded, result,
):
    task = pl.program_id(0)

    @pl.when(plan[task, 3] < 0)
    def _():
        out[...] = jnp.zeros_like(out)

    @pl.when(plan[task, 3] >= 0)
    def _():
        assemble(plan[task, 0], left_whole, left_cut, left)
        assemble(plan[task, 1], right_whole, right_cut, right)
        ladder_task(left, right, amp, swap, out, right_t, amp_t, integral, folded, result)


def ladder_task(left, right, amp, swap, out, right_t, amp_t, integral, folded, result):
    width = left.shape[1]
    occupied = amp.shape[1]
    per_pass = 2 * FOLD
    span = per_pass * VB
    right_t[...] = jnp.dot(right[...], swap[...], preferred_element_type=jnp.float32).astype(jnp.bfloat16)
    amp_t[...] = jnp.dot(amp[0], swap[...], preferred_element_type=jnp.float32).astype(jnp.bfloat16)

    def products(step, _):
        columns = pl.ds(pl.multiple_of(step * 2 * span, 2 * span), 2 * span)
        integral[columns, :] = lax.dot_general(
            left[:, columns], right_t[...], (((0,), (0,)), ((), ())), preferred_element_type=jnp.float32
        ).astype(jnp.bfloat16)
        return 0

    lax.fori_loop(0, VB // per_pass // 2, products, 0)

    def one_pass(step, _):
        columns = pl.ds(pl.multiple_of(step * span, span), span)
        for part in range(width // LANES):
            lanes = slice(part * LANES, (part + 1) * LANES)
            for half in range(2):
                rows = half * FOLD * VB
                tiles = [
                    integral[pl.ds(pl.multiple_of(step * span + rows + a * VB, VB), VB), lanes] for a in range(FOLD)
                ]
                for d, tile in enumerate(swap_lane_blocks(tiles)):
                    base = (part * FOLD + d) * VB
                    folded[base : base + VB, half * LANES : (half + 1) * LANES] = tile
        result[:, columns] = jnp.dot(amp_t[...], folded[...], preferred_element_type=jnp.float32)
        return 0

    lax.fori_loop(0, VB // per_pass, one_pass, 0)
    band = occupied // FOLD
    for group in range(width // LANES):
        lanes = slice(group * LANES, (group + 1) * LANES)
        tiles = [result[i * band : (i + 1) * band, lanes] for i in range(FOLD)]
        for a, tile in enumerate(swap_lane_blocks(tiles)):
            out[group * FOLD + a, 0] = tile.astype(out.dtype)


def ladder(plan, factors, arrived, amps):
    rows, width = factors.shape[1:]
    tasks, occupied = amps.shape[:2]
    index = jnp.arange(width, dtype=jnp.int32)
    swap = (
        (index[:, None] // VB == index[None, :] % VB) & (index[:, None] % VB == index[None, :] // VB)
    ).astype(jnp.bfloat16)
    band = occupied // FOLD
    pieces, _, piece_rows, _ = arrived.shape

    def whole(side):
        def place(k, plan):
            return jnp.where(plan[k, side] < FPG, plan[k, side], 0), 0, 0

        return pl.BlockSpec((1, rows, width), place)

    def cut(side):
        def place(k, plan):
            return 0, jnp.where(plan[k, side] < FPG, 0, plan[k, side] - FPG), 0, 0

        return pl.BlockSpec((pieces, 1, piece_rows, LANES), place)

    return pl.pallas_call(
        ladder_kernel,
        grid_spec=pltpu.PrefetchScalarGridSpec(
            num_scalar_prefetch=1,
            grid=(tasks,),
            in_specs=[
                whole(0),
                cut(0),
                whole(1),
                cut(1),
                pl.BlockSpec((1, occupied, width), lambda k, plan: (k, 0, 0)),
                pl.BlockSpec((width, width), lambda k, plan: (0, 0)),
            ],
            out_specs=pl.BlockSpec((VB, 1, band, LANES), lambda k, plan: (0, k, 0, 0)),
            scratch_shapes=[
                pltpu.VMEM((rows, width), jnp.bfloat16),
                pltpu.VMEM((rows, width), jnp.bfloat16),
                pltpu.VMEM((rows, width), jnp.bfloat16),
                pltpu.VMEM((occupied, width), jnp.bfloat16),
                pltpu.VMEM((width, width), jnp.bfloat16),
                pltpu.VMEM((width, 2 * LANES), jnp.bfloat16),
                pltpu.VMEM((occupied, width), jnp.float32),
            ],
        ),
        out_shape=jax.ShapeDtypeStruct((VB, tasks, band, LANES), jnp.bfloat16),
        compiler_params=pltpu.CompilerParams(dimension_semantics=("arbitrary",)),
        name="ladder",
    )(plan, factors, arrived, factors, arrived, amps, swap)


def combine_kernel(plan, pieces, out):
    total = jnp.sum(pieces[...].astype(jnp.float32), axis=0)
    out[...] = jnp.zeros_like(out)
    for k in range(pieces.shape[1]):
        target = plan[k, 3]

        @pl.when(target >= 0)
        def _():
            out[target] += total[k]


def combine(plan, pieces, tiles):
    return pl.pallas_call(
        combine_kernel,
        in_specs=[pl.BlockSpec(memory_space=pltpu.SMEM), pl.BlockSpec(memory_space=pltpu.VMEM)],
        out_specs=pl.BlockSpec(memory_space=pltpu.VMEM),
        out_shape=jax.ShapeDtypeStruct((tiles, *pieces.shape[2:]), jnp.float32),
        name="combine",
    )(plan, pieces)


def owned_kernel(arrived, out):
    groups, tiles, band, lanes = arrived.shape
    for t in range(tiles):
        total = jnp.sum(arrived[:, t], axis=0)
        for i in range(FOLD):
            out[t, i * band : (i + 1) * band, :] = total[:, i * VB : (i + 1) * VB]


def owned(arrived):
    groups, tiles, band, lanes = arrived.shape
    return pl.pallas_call(
        owned_kernel,
        in_specs=[pl.BlockSpec(memory_space=pltpu.VMEM)],
        out_specs=pl.BlockSpec(memory_space=pltpu.VMEM),
        out_shape=jax.ShapeDtypeStruct((tiles, band * FOLD, VB), jnp.float32),
        name="owned",
    )(arrived)


def assign_kernel(
    me, table, send, pick, plan, balanced,
    compute, other, compute_block, other_block, load, sent, uses, filled, slots, where_sent,
):
    groups = table.shape[0]
    mine = me[0]
    for g in range(groups):
        load[g] = 0
        sent[g] = 0
        filled[g] = 0
        slots[g] = 0

    def clear(i, _):
        for j in range(FPG):
            uses[i * FPG + j] = 0
            where_sent[i * FPG + j] = -1
            pick[i * FPG + j] = 0
        return 0

    lax.fori_loop(0, groups, clear, 0)
    for i in range(send.shape[0]):
        send[i] = 0
    for k in range(plan.shape[0]):
        for j in range(3):
            plan[k, j] = 0
        plan[k, 3] = -1

    def first_choice(h, _):
        for k in range(TASKS):
            s1, s2 = table[h, RECORDS + 4 * k + 1], table[h, RECORDS + 4 * k + 2]
            b1, b2 = table[s1, FACTOR_ROUTE + h], table[s2, FACTOR_ROUTE + h]
            n1, n2 = uses[s1 * FPG + b1], uses[s2 * FPG + b2]
            at_first = 2 * load[s1] - jnp.where(n2 > 0, 0, FAST - sent[s2])
            at_second = 2 * load[s2] - jnp.where(n1 > 0, 0, FAST - sent[s1])
            second = (at_first > at_second) & (s1 != s2)
            c, o = jnp.where(second, s2, s1), jnp.where(second, s1, s2)
            y, x = jnp.where(second, b2, b1), jnp.where(second, b1, b2)
            n = jnp.where(second, n1, n2)
            moved = jnp.where(c != o, 1, 0)
            i = h * TASKS + k
            compute[i], other[i], compute_block[i], other_block[i] = c, o, y, x
            load[c] += 1
            sent[o] += jnp.where(n == 0, moved, 0)
            uses[o * FPG + x] = n + moved
        return 0

    lax.fori_loop(0, groups, first_choice, 0)
    over = lambda n: jnp.maximum(n - FAST, 0)

    def excess():
        total = 0
        for g in range(groups):
            total += over(load[g]) + over(sent[g])
        return total

    def sweep(state):
        def visit(i, bad):
            c, o = compute[i], other[i]
            wanted = (c != o) & ((load[c] > FAST) | (sent[o] > FAST))

            def flip(bad):
                y, x = compute_block[i], other_block[i]
                nc, no = uses[c * FPG + y], uses[o * FPG + x]
                less, more = jnp.where(no == 1, 1, 0), jnp.where(nc == 0, 1, 0)
                lc, lo, sc, so = load[c], load[o], sent[c], sent[o]
                change = over(lc - 1) - over(lc) + over(lo + 1) - over(lo)
                change += over(sc + more) - over(sc) + over(so - less) - over(so)

                def take(bad):
                    compute[i], other[i], compute_block[i], other_block[i] = o, c, x, y
                    load[c], load[o] = lc - 1, lo + 1
                    sent[c], sent[o] = sc + more, so - less
                    uses[c * FPG + y], uses[o * FPG + x] = nc + 1, no - 1
                    return bad + change

                return lax.cond(change <= 0, take, lambda bad: bad, bad)

            return lax.cond(wanted, flip, lambda bad: bad, bad)

        return state[0] + 1, lax.fori_loop(0, groups * TASKS, visit, state[1])

    _, bad = lax.while_loop(lambda s: (s[0] < SWEEPS) & (s[1] > 0), sweep, (jnp.int32(0), excess()))
    good = bad == 0
    balanced[0] = jnp.where(good, 1, 0)
    stride = jnp.where(good, FAST, FPG)

    def fetch(source, block, c):
        remote = source != c
        known = where_sent[source * FPG + block]
        fresh = remote & (known < 0)
        count = filled[source]
        at = jnp.where(fresh, count, known)
        filled[source] = count + jnp.where(fresh, 1, 0)
        where_sent[source * FPG + block] = at
        send[jnp.where(fresh & (source == mine), at, FPG)] = block
        slot = slots[c]
        slots[c] = slot + jnp.where(remote, 1, 0)
        pick[jnp.where(remote, c * FPG + slot, groups * FPG)] = source * stride + at
        return jnp.where(remote, FPG + slot, block)

    def note(h, k, c, left, right):
        o, s3 = table[h, RECORDS + 4 * k], table[h, RECORDS + 4 * k + 3]
        t = load[c]
        load[c] = t + 1
        row = jnp.where(c == mine, t, FAST)
        plan[row, 0] = left
        plan[row, 1] = right
        plan[row, 2] = s3 * (APG + 1) + table[s3, h]
        plan[row, 3] = o * TPG + table[o, TARGET + h]

    def deal_balanced(h, _):
        for k in range(TASKS):
            i = h * TASKS + k
            c, y = compute[i], compute_block[i]
            found = fetch(other[i], other_block[i], c)
            first = c == table[h, RECORDS + 4 * k + 1]
            note(h, k, c, jnp.where(first, y, found), jnp.where(first, found, y))
        return 0

    def deal_at_helper(h, _):
        for k in range(TASKS):
            s1, s2 = table[h, RECORDS + 4 * k + 1], table[h, RECORDS + 4 * k + 2]
            left = fetch(s1, table[s1, FACTOR_ROUTE + h], h)
            right = fetch(s2, table[s2, FACTOR_ROUTE + h], h)
            note(h, k, h, left, right)
        return 0

    for g in range(groups):
        load[g] = 0

    @pl.when(good)
    def _():
        lax.fori_loop(0, groups, deal_balanced, 0)

    @pl.when(jnp.logical_not(good))
    def _():
        lax.fori_loop(0, groups, deal_at_helper, 0)


def assign(me, table):
    groups = table.shape[0]
    smem = pl.BlockSpec(memory_space=pltpu.SMEM)
    one = lambda n: pltpu.SMEM((n,), jnp.int32)
    tasks = groups * TASKS
    return pl.pallas_call(
        assign_kernel,
        in_specs=[smem, smem],
        out_specs=[smem] * 4,
        out_shape=[
            jax.ShapeDtypeStruct((2 * FPG,), jnp.int32),
            jax.ShapeDtypeStruct(((groups + 1) * FPG,), jnp.int32),
            jax.ShapeDtypeStruct((2 * FAST, 4), jnp.int32),
            jax.ShapeDtypeStruct((1,), jnp.int32),
        ],
        scratch_shapes=[one(tasks)] * 4 + [one(groups)] * 2 + [one(groups * FPG)] + [one(groups)] * 2 + [one(groups * FPG)],
        name="assign",
    )(me, table)


def cut_kernel(block, out):
    rows = out.shape[2]
    for piece in range(out.shape[0]):
        half, part = divmod(piece, block.shape[2] // LANES)
        out[piece, 0] = block[0, half * rows : (half + 1) * rows, part * LANES : (part + 1) * LANES]


def cut_blocks(factors, pieces):
    count, rows, width = factors.shape
    piece_rows = rows * width // LANES // pieces
    size = factors.size * 2
    return pl.pallas_call(
        cut_kernel,
        grid=(count,),
        in_specs=[pl.BlockSpec((1, rows, width), lambda i: (i, 0, 0))],
        out_specs=pl.BlockSpec((pieces, 1, piece_rows, LANES), lambda i: (0, i, 0, 0)),
        out_shape=jax.ShapeDtypeStruct((pieces, count, piece_rows, LANES), factors.dtype),
        compiler_params=pltpu.CompilerParams(dimension_semantics=("arbitrary",)),
        cost_estimate=pl.CostEstimate(flops=0, bytes_accessed=2 * size, transcendentals=0),
        name="cut_blocks",
    )(factors)


def spread(held, axis, bits):
    members = lax.axis_size(axis)
    me = lax.axis_index(axis)
    for bit in bits:
        other = lax.ppermute(held, axis, [(i, i ^ bit) for i in range(members)])
        mine_first = (me & bit) == 0
        held = jnp.where(
            mine_first, jnp.concatenate([held, other]), jnp.concatenate([other, held])
        )
    return held


def facts_kernel(shard, amplitudes, amp_route, factor_route, target_tile, task_list, out):
    tiles, occupied, width = amplitudes.shape
    chosen = lax.broadcasted_iota(jnp.int32, (occupied, width), 0) == shard[0]
    facts = [amp_route[...], factor_route[...], target_tile[...]]
    facts += [task_list[0, k : k + 1, :] for k in range(TASKS)]
    facts = jnp.concatenate(facts, axis=1).astype(jnp.float32)
    facts = jnp.concatenate([facts, jnp.zeros((1, LANES - facts.shape[1]), jnp.float32)], axis=1)
    parts = width // LANES
    for i in range(tiles + 1):
        if i < tiles:
            row = jnp.sum(jnp.where(chosen, amplitudes[i].astype(jnp.float32), 0.0), axis=0, keepdims=True)
            rows = [row[:, c * LANES : (c + 1) * LANES] for c in range(parts)]
        else:
            rows = [facts] + [jnp.zeros_like(facts)] * (parts - 1)
        tile = jnp.concatenate(rows, axis=0).astype(out.dtype)
        for g in range(out.shape[0]):
            out[g, i] = tile


def group_facts(amplitudes, factor_route, amp_route, task_list, target_tile):
    groups = lax.axis_size("group")
    tiles, _, width = amplitudes.shape
    shard = lax.axis_index("shard").astype(jnp.int32).reshape(1)
    vmem = pl.BlockSpec(memory_space=pltpu.VMEM)
    facts = pl.pallas_call(
        facts_kernel,
        in_specs=[pl.BlockSpec(memory_space=pltpu.SMEM)] + [vmem] * 5,
        out_specs=vmem,
        out_shape=jax.ShapeDtypeStruct((groups, tiles + 1, width // LANES, LANES), amplitudes.dtype),
        name="facts",
    )(shard, amplitudes, amp_route, factor_route, target_tile, task_list)
    held = lax.all_to_all(facts, "group", split_axis=0, concat_axis=0, tiled=True)
    return held.reshape(groups * (tiles + 1), *held.shape[2:]), held[:, tiles, 0].astype(jnp.int32)


def contributions(blocks_sent, slots, factors, cut, amp_rows, send, pick, plan):
    groups, count = cut.shape[:2]
    width = factors.shape[2]
    piece = cut.shape[2:]
    order = jnp.arange(groups, dtype=jnp.int32)[:, None] * count + send[None, :blocks_sent]
    leaving = cut.reshape(groups * count, *piece).at[order.reshape(-1)].get(mode="promise_in_bounds")
    leaving = leaving.reshape(groups, blocks_sent, *piece)
    held = lax.all_to_all(leaving, "group", split_axis=0, concat_axis=0, tiled=True)
    chosen = amp_rows.at[plan[:FAST, 2]].get(mode="promise_in_bounds")
    amps = spread(chosen[None], "shard", (1, 2, 4))
    held, amps = lax.optimization_barrier((held, amps))
    wanted = pick[: groups * FPG].reshape(groups, FPG)[:, :slots].reshape(-1)
    dealt = held.reshape(groups * blocks_sent, *piece).at[wanted].get(mode="promise_in_bounds")
    dealt = dealt.reshape(groups, slots, *piece)
    arrived = lax.all_to_all(dealt, "group", split_axis=0, concat_axis=0, tiled=True)
    amps = spread(amps, "shard", (8, 16))
    amps = amps.reshape(-1, FAST, width).transpose(1, 0, 2)
    return ladder(plan, factors, arrived, amps)


def body(factors, amplitudes, factor_route, amp_route, task_list, target_tile):
    groups = lax.axis_size("group")
    amp_rows, table = group_facts(amplitudes, factor_route, amp_route, task_list, target_tile)
    cut = cut_blocks(factors, groups)
    me = lax.axis_index("group").astype(jnp.int32).reshape(1)
    send, pick, plan, balanced = assign(me, table)
    operands = (factors, cut, amp_rows, send, pick, plan)
    parts = lax.cond(
        balanced[0] == 1,
        functools.partial(contributions, FAST, FAST),
        functools.partial(contributions, FPG, 2 * TASKS),
        *operands,
    )
    pieces = lax.all_to_all(parts, "shard", split_axis=0, concat_axis=0, tiled=True)
    returns = combine(plan, pieces, groups * TPG)
    arrived = lax.all_to_all(returns, "group", split_axis=0, concat_axis=0, tiled=True)
    return owned(arrived.reshape(groups, TPG, *arrived.shape[1:]))


def solution(mesh):
    return jax.shard_map(
        body,
        mesh=mesh,
        in_specs=(
            P("group", "shard", None),
            P("group", None, None),
            P("group", None),
            P("group", None),
            P("group", None, None),
            P("group", None),
        ),
        out_specs=P("group", None, "shard"),
        check_vma=False,
    )
```

```python
import functools

import jax
import jax.numpy as jnp
from jax import lax
from jax.experimental import pallas as pl
from jax.experimental.pallas import tpu as pltpu
from jax.sharding import PartitionSpec as P

VB = 32
FPG = 8
APG = 4
TPG = 2
TASKS = 3
LANES = 128
FAST = 4
SWEEPS = 12
FACTOR_ROUTE, TARGET, RECORDS = 16, 32, 48
FOLD = LANES // VB


def swap_lane_blocks(tiles):
    lane = lax.broadcasted_iota(jnp.int32, tiles[0].shape, 1)
    low = lane.astype(tiles[0].dtype) < 2 * VB
    even = (lane % (2 * VB)).astype(tiles[0].dtype) < VB
    x0, x1, x2, x3 = tiles
    y0 = jnp.where(low, x0, pltpu.roll(x2, 2 * VB, 1))
    y2 = jnp.where(low, pltpu.roll(x0, 2 * VB, 1), x2)
    y1 = jnp.where(low, x1, pltpu.roll(x3, 2 * VB, 1))
    y3 = jnp.where(low, pltpu.roll(x1, 2 * VB, 1), x3)
    z0 = jnp.where(even, y0, pltpu.roll(y1, VB, 1))
    z1 = jnp.where(even, pltpu.roll(y0, LANES - VB, 1), y1)
    z2 = jnp.where(even, y2, pltpu.roll(y3, VB, 1))
    z3 = jnp.where(even, pltpu.roll(y2, LANES - VB, 1), y3)
    return z0, z1, z2, z3


def assemble(select, whole, cut, out):
    @pl.when(select < FPG)
    def _():
        out[...] = whole[0]

    @pl.when(select >= FPG)
    def _():
        rows = cut.shape[2]
        for piece in range(cut.shape[0]):
            half, part = divmod(piece, out.shape[1] // LANES)
            out[half * rows : (half + 1) * rows, part * LANES : (part + 1) * LANES] = cut[piece, 0]


def ladder_kernel(
    plan, left_whole, left_cut, right_whole, right_cut, amp, swap, out,
    left, right, right_t, amp_t, integral, folded, result,
):
    task = pl.program_id(0)

    @pl.when(plan[task, 3] < 0)
    def _():
        out[...] = jnp.zeros_like(out)

    @pl.when(plan[task, 3] >= 0)
    def _():
        assemble(plan[task, 0], left_whole, left_cut, left)
        assemble(plan[task, 1], right_whole, right_cut, right)
        ladder_task(left, right, amp, swap, out, right_t, amp_t, integral, folded, result)


def ladder_task(left, right, amp, swap, out, right_t, amp_t, integral, folded, result):
    width = left.shape[1]
    occupied = amp.shape[1]
    per_pass = 2 * FOLD
    span = per_pass * VB
    right_t[...] = jnp.dot(right[...], swap[...], preferred_element_type=jnp.float32).astype(jnp.bfloat16)
    amp_t[...] = jnp.dot(amp[0], swap[...], preferred_element_type=jnp.float32).astype(jnp.bfloat16)

    def products(step, _):
        columns = pl.ds(pl.multiple_of(step * 2 * span, 2 * span), 2 * span)
        integral[columns, :] = lax.dot_general(
            left[:, columns], right_t[...], (((0,), (0,)), ((), ())), preferred_element_type=jnp.float32
        ).astype(jnp.bfloat16)
        return 0

    lax.fori_loop(0, VB // per_pass // 2, products, 0)

    def one_pass(step, _):
        columns = pl.ds(pl.multiple_of(step * span, span), span)
        for part in range(width // LANES):
            lanes = slice(part * LANES, (part + 1) * LANES)
            for half in range(2):
                rows = half * FOLD * VB
                tiles = [
                    integral[pl.ds(pl.multiple_of(step * span + rows + a * VB, VB), VB), lanes] for a in range(FOLD)
                ]
                for d, tile in enumerate(swap_lane_blocks(tiles)):
                    base = (part * FOLD + d) * VB
                    folded[base : base + VB, half * LANES : (half + 1) * LANES] = tile
        result[:, columns] = jnp.dot(amp_t[...], folded[...], preferred_element_type=jnp.float32)
        return 0

    lax.fori_loop(0, VB // per_pass, one_pass, 0)
    band = occupied // FOLD
    for group in range(width // LANES):
        lanes = slice(group * LANES, (group + 1) * LANES)
        tiles = [result[i * band : (i + 1) * band, lanes] for i in range(FOLD)]
        for a, tile in enumerate(swap_lane_blocks(tiles)):
            out[group * FOLD + a, 0] = tile.astype(out.dtype)


def ladder(plan, factors, arrived, amps):
    rows, width = factors.shape[1:]
    tasks, occupied = amps.shape[:2]
    index = jnp.arange(width, dtype=jnp.int32)
    swap = (
        (index[:, None] // VB == index[None, :] % VB) & (index[:, None] % VB == index[None, :] // VB)
    ).astype(jnp.bfloat16)
    band = occupied // FOLD
    pieces, _, piece_rows, _ = arrived.shape

    def whole(side):
        def place(k, plan):
            return jnp.where(plan[k, side] < FPG, plan[k, side], 0), 0, 0

        return pl.BlockSpec((1, rows, width), place)

    def cut(side):
        def place(k, plan):
            return 0, jnp.where(plan[k, side] < FPG, 0, plan[k, side] - FPG), 0, 0

        return pl.BlockSpec((pieces, 1, piece_rows, LANES), place)

    return pl.pallas_call(
        ladder_kernel,
        grid_spec=pltpu.PrefetchScalarGridSpec(
            num_scalar_prefetch=1,
            grid=(tasks,),
            in_specs=[
                whole(0),
                cut(0),
                whole(1),
                cut(1),
                pl.BlockSpec((1, occupied, width), lambda k, plan: (k, 0, 0)),
                pl.BlockSpec((width, width), lambda k, plan: (0, 0)),
            ],
            out_specs=pl.BlockSpec((VB, 1, band, LANES), lambda k, plan: (0, k, 0, 0)),
            scratch_shapes=[
                pltpu.VMEM((rows, width), jnp.bfloat16),
                pltpu.VMEM((rows, width), jnp.bfloat16),
                pltpu.VMEM((rows, width), jnp.bfloat16),
                pltpu.VMEM((occupied, width), jnp.bfloat16),
                pltpu.VMEM((width, width), jnp.bfloat16),
                pltpu.VMEM((width, 2 * LANES), jnp.bfloat16),
                pltpu.VMEM((occupied, width), jnp.float32),
            ],
        ),
        out_shape=jax.ShapeDtypeStruct((VB, tasks, band, LANES), jnp.bfloat16),
        compiler_params=pltpu.CompilerParams(dimension_semantics=("arbitrary",)),
        name="ladder",
    )(plan, factors, arrived, factors, arrived, amps, swap)


def combine_kernel(plan, pieces, out):
    total = jnp.sum(pieces[...].astype(jnp.float32), axis=0)
    out[...] = jnp.zeros_like(out)
    for k in range(pieces.shape[1]):
        target = plan[k, 3]

        @pl.when(target >= 0)
        def _():
            out[target] += total[k]


def combine(plan, pieces, tiles):
    return pl.pallas_call(
        combine_kernel,
        in_specs=[pl.BlockSpec(memory_space=pltpu.SMEM), pl.BlockSpec(memory_space=pltpu.VMEM)],
        out_specs=pl.BlockSpec(memory_space=pltpu.VMEM),
        out_shape=jax.ShapeDtypeStruct((tiles, *pieces.shape[2:]), jnp.float32),
        name="combine",
    )(plan, pieces)


def owned_kernel(arrived, out):
    groups, tiles, band, lanes = arrived.shape
    for t in range(tiles):
        total = jnp.sum(arrived[:, t], axis=0)
        for i in range(FOLD):
            out[t, i * band : (i + 1) * band, :] = total[:, i * VB : (i + 1) * VB]


def owned(arrived):
    groups, tiles, band, lanes = arrived.shape
    return pl.pallas_call(
        owned_kernel,
        in_specs=[pl.BlockSpec(memory_space=pltpu.VMEM)],
        out_specs=pl.BlockSpec(memory_space=pltpu.VMEM),
        out_shape=jax.ShapeDtypeStruct((tiles, band * FOLD, VB), jnp.float32),
        name="owned",
    )(arrived)


def assign_kernel(
    me, table, send, pick, plan, balanced,
    compute, other, compute_block, other_block, load, sent, uses, filled, slots, where_sent,
):
    groups = table.shape[0]
    mine = me[0]
    for g in range(groups):
        load[g] = 0
        sent[g] = 0
        filled[g] = 0
        slots[g] = 0

    def clear(i, _):
        for j in range(FPG):
            uses[i * FPG + j] = 0
            where_sent[i * FPG + j] = -1
            pick[i * FPG + j] = 0
        return 0

    lax.fori_loop(0, groups, clear, 0)
    for i in range(send.shape[0]):
        send[i] = 0
    for k in range(plan.shape[0]):
        for j in range(3):
            plan[k, j] = 0
        plan[k, 3] = -1

    def first_choice(h, _):
        for k in range(TASKS):
            s1, s2 = table[h, RECORDS + 4 * k + 1], table[h, RECORDS + 4 * k + 2]
            b1, b2 = table[s1, FACTOR_ROUTE + h], table[s2, FACTOR_ROUTE + h]
            n1, n2 = uses[s1 * FPG + b1], uses[s2 * FPG + b2]
            at_first = 2 * load[s1] - jnp.where(n2 > 0, 0, FAST - sent[s2])
            at_second = 2 * load[s2] - jnp.where(n1 > 0, 0, FAST - sent[s1])
            second = (at_first > at_second) & (s1 != s2)
            c, o = jnp.where(second, s2, s1), jnp.where(second, s1, s2)
            y, x = jnp.where(second, b2, b1), jnp.where(second, b1, b2)
            n = jnp.where(second, n1, n2)
            moved = jnp.where(c != o, 1, 0)
            i = h * TASKS + k
            compute[i], other[i], compute_block[i], other_block[i] = c, o, y, x
            load[c] += 1
            sent[o] += jnp.where(n == 0, moved, 0)
            uses[o * FPG + x] = n + moved
        return 0

    lax.fori_loop(0, groups, first_choice, 0)
    over = lambda n: jnp.maximum(n - FAST, 0)

    def excess():
        total = 0
        for g in range(groups):
            total += over(load[g]) + over(sent[g])
        return total

    def sweep(state):
        def visit(i, bad):
            c, o = compute[i], other[i]
            wanted = (c != o) & ((load[c] > FAST) | (sent[o] > FAST))

            def flip(bad):
                y, x = compute_block[i], other_block[i]
                nc, no = uses[c * FPG + y], uses[o * FPG + x]
                less, more = jnp.where(no == 1, 1, 0), jnp.where(nc == 0, 1, 0)
                lc, lo, sc, so = load[c], load[o], sent[c], sent[o]
                change = over(lc - 1) - over(lc) + over(lo + 1) - over(lo)
                change += over(sc + more) - over(sc) + over(so - less) - over(so)

                def take(bad):
                    compute[i], other[i], compute_block[i], other_block[i] = o, c, x, y
                    load[c], load[o] = lc - 1, lo + 1
                    sent[c], sent[o] = sc + more, so - less
                    uses[c * FPG + y], uses[o * FPG + x] = nc + 1, no - 1
                    return bad + change

                return lax.cond(change <= 0, take, lambda bad: bad, bad)

            return lax.cond(wanted, flip, lambda bad: bad, bad)

        return state[0] + 1, lax.fori_loop(0, groups * TASKS, visit, state[1])

    _, bad = lax.while_loop(lambda s: (s[0] < SWEEPS) & (s[1] > 0), sweep, (jnp.int32(0), excess()))
    good = bad == 0
    balanced[0] = jnp.where(good, 1, 0)
    stride = jnp.where(good, FAST, FPG)

    def fetch(source, block, c):
        remote = source != c
        known = where_sent[source * FPG + block]
        fresh = remote & (known < 0)
        count = filled[source]
        at = jnp.where(fresh, count, known)
        filled[source] = count + jnp.where(fresh, 1, 0)
        where_sent[source * FPG + block] = at
        send[jnp.where(fresh & (source == mine), at, FPG)] = block
        slot = slots[c]
        slots[c] = slot + jnp.where(remote, 1, 0)
        pick[jnp.where(remote, c * FPG + slot, groups * FPG)] = source * stride + at
        return jnp.where(remote, FPG + slot, block)

    def note(h, k, c, left, right):
        o, s3 = table[h, RECORDS + 4 * k], table[h, RECORDS + 4 * k + 3]
        t = load[c]
        load[c] = t + 1
        row = jnp.where(c == mine, t, FAST)
        plan[row, 0] = left
        plan[row, 1] = right
        plan[row, 2] = s3 * (APG + 1) + table[s3, h]
        plan[row, 3] = o * TPG + table[o, TARGET + h]

    def deal_balanced(h, _):
        for k in range(TASKS):
            i = h * TASKS + k
            c, y = compute[i], compute_block[i]
            found = fetch(other[i], other_block[i], c)
            first = c == table[h, RECORDS + 4 * k + 1]
            note(h, k, c, jnp.where(first, y, found), jnp.where(first, found, y))
        return 0

    def deal_at_helper(h, _):
        for k in range(TASKS):
            s1, s2 = table[h, RECORDS + 4 * k + 1], table[h, RECORDS + 4 * k + 2]
            left = fetch(s1, table[s1, FACTOR_ROUTE + h], h)
            right = fetch(s2, table[s2, FACTOR_ROUTE + h], h)
            note(h, k, h, left, right)
        return 0

    for g in range(groups):
        load[g] = 0

    @pl.when(good)
    def _():
        lax.fori_loop(0, groups, deal_balanced, 0)

    @pl.when(jnp.logical_not(good))
    def _():
        lax.fori_loop(0, groups, deal_at_helper, 0)


def assign(me, table):
    groups = table.shape[0]
    smem = pl.BlockSpec(memory_space=pltpu.SMEM)
    one = lambda n: pltpu.SMEM((n,), jnp.int32)
    tasks = groups * TASKS
    return pl.pallas_call(
        assign_kernel,
        in_specs=[smem, smem],
        out_specs=[smem] * 4,
        out_shape=[
            jax.ShapeDtypeStruct((2 * FPG,), jnp.int32),
            jax.ShapeDtypeStruct(((groups + 1) * FPG,), jnp.int32),
            jax.ShapeDtypeStruct((2 * FAST, 4), jnp.int32),
            jax.ShapeDtypeStruct((1,), jnp.int32),
        ],
        scratch_shapes=[one(tasks)] * 4 + [one(groups)] * 2 + [one(groups * FPG)] + [one(groups)] * 2 + [one(groups * FPG)],
        name="assign",
    )(me, table)


def leave_kernel(send, factors, out, held, arrive, leave):
    pieces, count, rows, _ = out.shape
    width = factors.shape[2]
    blocks = [pltpu.make_async_copy(factors.at[send[i]], held.at[i], arrive.at[i]) for i in range(count)]
    parts = []
    for block in blocks:
        block.start()
    for i, block in enumerate(blocks):
        block.wait()
        for piece in range(pieces):
            half, part = divmod(piece, width // LANES)
            piece_of = held.at[i, half * rows : (half + 1) * rows, part * LANES : (part + 1) * LANES]
            parts.append(pltpu.make_async_copy(piece_of, out.at[piece, i], leave.at[i * pieces + piece]))
            parts[-1].start()
    for part in parts:
        part.wait()


def leaving_pieces(send, factors, count, pieces):
    _, rows, width = factors.shape
    piece_rows = rows * width // LANES // pieces
    return pl.pallas_call(
        leave_kernel,
        in_specs=[pl.BlockSpec(memory_space=pltpu.SMEM), pl.BlockSpec(memory_space=pl.ANY)],
        out_specs=pl.BlockSpec(memory_space=pl.ANY),
        out_shape=jax.ShapeDtypeStruct((pieces, count, piece_rows, LANES), factors.dtype),
        scratch_shapes=[
            pltpu.VMEM((count, rows, width), factors.dtype),
            pltpu.SemaphoreType.DMA((count,)),
            pltpu.SemaphoreType.DMA((count * pieces,)),
        ],
        name="leaving_pieces",
    )(send, factors)


def deal_kernel(pick, pieces, out, held, arrive, leave):
    groups, slots = out.shape[:2]
    whole = pltpu.make_async_copy(pieces, held, arrive)
    whole.start()
    whole.wait()
    parts = []
    for g in range(groups):
        for j in range(slots):
            source = held.at[pick[g * FPG + j]]
            parts.append(pltpu.make_async_copy(source, out.at[g, j], leave.at[g * slots + j]))
            parts[-1].start()
    for part in parts:
        part.wait()


def dealt_pieces(pick, pieces, groups, slots):
    count, rows, lanes = pieces.shape
    return pl.pallas_call(
        deal_kernel,
        in_specs=[pl.BlockSpec(memory_space=pltpu.SMEM), pl.BlockSpec(memory_space=pl.ANY)],
        out_specs=pl.BlockSpec(memory_space=pl.ANY),
        out_shape=jax.ShapeDtypeStruct((groups, slots, rows, lanes), pieces.dtype),
        scratch_shapes=[
            pltpu.VMEM(pieces.shape, pieces.dtype),
            pltpu.SemaphoreType.DMA,
            pltpu.SemaphoreType.DMA((groups * slots,)),
        ],
        name="dealt_pieces",
    )(pick, pieces)


def spread(held, axis, bits):
    members = lax.axis_size(axis)
    me = lax.axis_index(axis)
    for bit in bits:
        other = lax.ppermute(held, axis, [(i, i ^ bit) for i in range(members)])
        mine_first = (me & bit) == 0
        held = jnp.where(
            mine_first, jnp.concatenate([held, other]), jnp.concatenate([other, held])
        )
    return held


def facts_kernel(shard, amplitudes, amp_route, factor_route, target_tile, task_list, out):
    tiles, occupied, width = amplitudes.shape
    chosen = lax.broadcasted_iota(jnp.int32, (occupied, width), 0) == shard[0]
    facts = [amp_route[...], factor_route[...], target_tile[...]]
    facts += [task_list[k] for k in range(TASKS)]
    facts = jnp.concatenate(facts, axis=1).astype(jnp.float32)
    facts = jnp.concatenate([facts, jnp.zeros((1, LANES - facts.shape[1]), jnp.float32)], axis=1)
    parts = width // LANES
    for i in range(tiles + 1):
        if i < tiles:
            row = jnp.sum(jnp.where(chosen, amplitudes[i].astype(jnp.float32), 0.0), axis=0, keepdims=True)
            rows = [row[:, c * LANES : (c + 1) * LANES] for c in range(parts)]
        else:
            rows = [facts] + [jnp.zeros_like(facts)] * (parts - 1)
        tile = jnp.concatenate(rows, axis=0).astype(out.dtype)
        for g in range(out.shape[0]):
            out[g, i] = tile


def group_facts(amplitudes, factor_route, amp_route, task_list, target_tile):
    groups = lax.axis_size("group")
    tiles, _, width = amplitudes.shape
    shard = lax.axis_index("shard").astype(jnp.int32).reshape(1)
    vmem = pl.BlockSpec(memory_space=pltpu.VMEM)
    facts = pl.pallas_call(
        facts_kernel,
        in_specs=[pl.BlockSpec(memory_space=pltpu.SMEM)] + [vmem] * 5,
        out_specs=vmem,
        out_shape=jax.ShapeDtypeStruct((groups, tiles + 1, width // LANES, LANES), amplitudes.dtype),
        name="facts",
    )(shard, amplitudes, amp_route, factor_route, target_tile, task_list.transpose(1, 0, 2))
    held = lax.all_to_all(facts, "group", split_axis=0, concat_axis=0, tiled=True)
    return held.reshape(groups * (tiles + 1), *held.shape[2:]), held[:, tiles, 0].astype(jnp.int32)


def contributions(blocks_sent, slots, factors, amp_rows, send, pick, plan):
    groups = lax.axis_size("group")
    width = factors.shape[2]
    leaving = leaving_pieces(send, factors, blocks_sent, groups)
    held = lax.all_to_all(leaving, "group", split_axis=0, concat_axis=0, tiled=True)
    chosen = amp_rows.at[plan[:FAST, 2]].get(mode="promise_in_bounds")
    amps = spread(chosen[None], "shard", (1, 2, 4))
    held, amps = lax.optimization_barrier((held, amps))
    dealt = dealt_pieces(pick, held.reshape(groups * blocks_sent, *held.shape[2:]), groups, slots)
    arrived = lax.all_to_all(dealt, "group", split_axis=0, concat_axis=0, tiled=True)
    amps = spread(amps, "shard", (8, 16))
    amps = amps.reshape(-1, FAST, width).transpose(1, 0, 2)
    return ladder(plan, factors, arrived, amps)


def body(factors, amplitudes, factor_route, amp_route, task_list, target_tile):
    groups = lax.axis_size("group")
    amp_rows, table = group_facts(amplitudes, factor_route, amp_route, task_list, target_tile)
    me = lax.axis_index("group").astype(jnp.int32).reshape(1)
    send, pick, plan, balanced = assign(me, table)
    operands = (factors, amp_rows, send, pick, plan)
    parts = lax.cond(
        balanced[0] == 1,
        functools.partial(contributions, FAST, FAST),
        functools.partial(contributions, FPG, 2 * TASKS),
        *operands,
    )
    pieces = lax.all_to_all(parts, "shard", split_axis=0, concat_axis=0, tiled=True)
    returns = combine(plan, pieces, groups * TPG)
    arrived = lax.all_to_all(returns, "group", split_axis=0, concat_axis=0, tiled=True)
    return owned(arrived.reshape(groups, TPG, *arrived.shape[1:]))


def solution(mesh):
    return jax.shard_map(
        body,
        mesh=mesh,
        in_specs=(
            P("group", "shard", None),
            P("group", None, None),
            P("group", None),
            P("group", None),
            P("group", None, None),
            P("group", None),
        ),
        out_specs=P("group", None, "shard"),
        check_vma=False,
    )
```

```python
import functools

import jax
import jax.numpy as jnp
from jax import lax
from jax.experimental import pallas as pl
from jax.experimental.pallas import tpu as pltpu
from jax.sharding import PartitionSpec as P

VB = 32
FPG = 8
APG = 4
TPG = 2
TASKS = 3
LANES = 128
FAST = 4
SWEEPS = 12
FACTOR_ROUTE, TARGET, RECORDS = 16, 32, 48
FOLD = LANES // VB


def swap_lane_blocks(tiles, unit):
    lane = lax.broadcasted_iota(jnp.int32, tiles[0].shape, 1)
    low = (lane % (4 * unit)).astype(tiles[0].dtype) < 2 * unit
    even = (lane % (2 * unit)).astype(tiles[0].dtype) < unit
    x0, x1, x2, x3 = tiles
    y0 = jnp.where(low, x0, pltpu.roll(x2, 2 * unit, 1))
    y2 = jnp.where(low, pltpu.roll(x0, LANES - 2 * unit, 1), x2)
    y1 = jnp.where(low, x1, pltpu.roll(x3, 2 * unit, 1))
    y3 = jnp.where(low, pltpu.roll(x1, LANES - 2 * unit, 1), x3)
    z0 = jnp.where(even, y0, pltpu.roll(y1, unit, 1))
    z1 = jnp.where(even, pltpu.roll(y0, LANES - unit, 1), y1)
    z2 = jnp.where(even, y2, pltpu.roll(y3, unit, 1))
    z3 = jnp.where(even, pltpu.roll(y2, LANES - unit, 1), y3)
    return z0, z1, z2, z3


def swap_pairs(source, swap, out):
    count, width = source.shape
    span = swap.shape[0]
    for group in range(width // span):
        columns = slice(group * span, (group + 1) * span)
        out[:, columns] = jnp.dot(source[:, columns], swap[...], preferred_element_type=jnp.float32).astype(out.dtype)
    for chunk in range(count // VB):
        rows = slice(chunk * VB, (chunk + 1) * VB)
        for odd in range(2):
            lanes = [slice((2 * i + odd) * LANES, (2 * i + odd + 1) * LANES) for i in range(FOLD)]
            tiles = swap_lane_blocks([out[rows, at] for at in lanes], VB // FOLD)
            for at, tile in zip(lanes, tiles):
                out[rows, at] = tile


def assemble(select, whole, cut, out):
    @pl.when(select < FPG)
    def _():
        out[...] = whole[0]

    @pl.when(select >= FPG)
    def _():
        rows = cut.shape[2]
        for piece in range(cut.shape[0]):
            half, part = divmod(piece, out.shape[1] // LANES)
            out[half * rows : (half + 1) * rows, part * LANES : (part + 1) * LANES] = cut[piece, 0]


def ladder_kernel(
    plan, left_whole, left_cut, right_whole, right_cut, amp, swap, out,
    left, right, right_t, amp_t, integral, folded, result,
):
    task = pl.program_id(0)

    @pl.when(plan[task, 3] < 0)
    def _():
        out[...] = jnp.zeros_like(out)

    @pl.when(plan[task, 3] >= 0)
    def _():
        assemble(plan[task, 0], left_whole, left_cut, left)
        assemble(plan[task, 1], right_whole, right_cut, right)
        ladder_task(left, right, amp, swap, out, right_t, amp_t, integral, folded, result)


def ladder_task(left, right, amp, swap, out, right_t, amp_t, integral, folded, result):
    width = left.shape[1]
    occupied = amp.shape[1]
    per_pass = 2 * FOLD
    span = per_pass * VB
    swap_pairs(right, swap, right_t)
    swap_pairs(amp.at[0], swap, amp_t)

    def products(step, _):
        columns = pl.ds(pl.multiple_of(step * 2 * span, 2 * span), 2 * span)
        integral[columns, :] = lax.dot_general(
            left[:, columns], right_t[...], (((0,), (0,)), ((), ())), preferred_element_type=jnp.float32
        ).astype(jnp.bfloat16)
        return 0

    lax.fori_loop(0, VB // per_pass // 2, products, 0)

    def one_pass(step, _):
        columns = pl.ds(pl.multiple_of(step * span, span), span)
        for part in range(width // LANES):
            lanes = slice(part * LANES, (part + 1) * LANES)
            for half in range(2):
                rows = half * FOLD * VB
                tiles = [
                    integral[pl.ds(pl.multiple_of(step * span + rows + a * VB, VB), VB), lanes] for a in range(FOLD)
                ]
                for d, tile in enumerate(swap_lane_blocks(tiles, VB)):
                    base = (part * FOLD + d) * VB
                    folded[base : base + VB, half * LANES : (half + 1) * LANES] = tile
        result[:, columns] = jnp.dot(amp_t[...], folded[...], preferred_element_type=jnp.float32)
        return 0

    lax.fori_loop(0, VB // per_pass, one_pass, 0)
    band = occupied // FOLD
    for group in range(width // LANES):
        lanes = slice(group * LANES, (group + 1) * LANES)
        tiles = [result[i * band : (i + 1) * band, lanes] for i in range(FOLD)]
        for a, tile in enumerate(swap_lane_blocks(tiles, VB)):
            out[group * FOLD + a, 0] = tile.astype(out.dtype)


def ladder(plan, factors, arrived, amps):
    rows, width = factors.shape[1:]
    tasks, occupied = amps.shape[:2]
    span = 2 * LANES
    index = jnp.arange(span, dtype=jnp.int32)
    p, q = index // VB, index % VB
    swap = ((q % 8 * VB + q // 8 * 8 + p)[:, None] == index[None, :]).astype(jnp.bfloat16)
    band = occupied // FOLD
    pieces, _, piece_rows, _ = arrived.shape

    def whole(side):
        def place(k, plan):
            return jnp.where(plan[k, side] < FPG, plan[k, side], 0), 0, 0

        return pl.BlockSpec((1, rows, width), place)

    def cut(side):
        def place(k, plan):
            return 0, jnp.where(plan[k, side] < FPG, 0, plan[k, side] - FPG), 0, 0

        return pl.BlockSpec((pieces, 1, piece_rows, LANES), place)

    return pl.pallas_call(
        ladder_kernel,
        grid_spec=pltpu.PrefetchScalarGridSpec(
            num_scalar_prefetch=1,
            grid=(tasks,),
            in_specs=[
                whole(0),
                cut(0),
                whole(1),
                cut(1),
                pl.BlockSpec((1, occupied, width), lambda k, plan: (k, 0, 0)),
                pl.BlockSpec((span, span), lambda k, plan: (0, 0)),
            ],
            out_specs=pl.BlockSpec((VB, 1, band, LANES), lambda k, plan: (0, k, 0, 0)),
            scratch_shapes=[
                pltpu.VMEM((rows, width), jnp.bfloat16),
                pltpu.VMEM((rows, width), jnp.bfloat16),
                pltpu.VMEM((rows, width), jnp.bfloat16),
                pltpu.VMEM((occupied, width), jnp.bfloat16),
                pltpu.VMEM((width, width), jnp.bfloat16),
                pltpu.VMEM((width, 2 * LANES), jnp.bfloat16),
                pltpu.VMEM((occupied, width), jnp.float32),
            ],
        ),
        out_shape=jax.ShapeDtypeStruct((VB, tasks, band, LANES), jnp.bfloat16),
        compiler_params=pltpu.CompilerParams(dimension_semantics=("arbitrary",)),
        name="ladder",
    )(plan, factors, arrived, factors, arrived, amps, swap)


def combine_kernel(plan, pieces, out):
    total = jnp.sum(pieces[...].astype(jnp.float32), axis=0)
    out[...] = jnp.zeros_like(out)
    for k in range(pieces.shape[1]):
        target = plan[k, 3]

        @pl.when(target >= 0)
        def _():
            out[target] += total[k]


def combine(plan, pieces, tiles):
    return pl.pallas_call(
        combine_kernel,
        in_specs=[pl.BlockSpec(memory_space=pltpu.SMEM), pl.BlockSpec(memory_space=pltpu.VMEM)],
        out_specs=pl.BlockSpec(memory_space=pltpu.VMEM),
        out_shape=jax.ShapeDtypeStruct((tiles, *pieces.shape[2:]), jnp.float32),
        name="combine",
    )(plan, pieces)


def owned_kernel(arrived, out):
    groups, tiles, band, lanes = arrived.shape
    for t in range(tiles):
        total = jnp.sum(arrived[:, t], axis=0)
        for i in range(FOLD):
            out[t, i * band : (i + 1) * band, :] = total[:, i * VB : (i + 1) * VB]


def owned(arrived):
    groups, tiles, band, lanes = arrived.shape
    return pl.pallas_call(
        owned_kernel,
        in_specs=[pl.BlockSpec(memory_space=pltpu.VMEM)],
        out_specs=pl.BlockSpec(memory_space=pltpu.VMEM),
        out_shape=jax.ShapeDtypeStruct((tiles, band * FOLD, VB), jnp.float32),
        name="owned",
    )(arrived)


def assign_kernel(
    me, table, send, pick, plan, balanced,
    compute, other, compute_block, other_block, load, sent, uses, filled, slots, where_sent,
):
    groups = table.shape[0]
    mine = me[0]
    for g in range(groups):
        load[g] = 0
        sent[g] = 0
        filled[g] = 0
        slots[g] = 0

    def clear(i, _):
        for j in range(FPG):
            uses[i * FPG + j] = 0
            where_sent[i * FPG + j] = -1
            pick[i * FPG + j] = 0
        return 0

    lax.fori_loop(0, groups, clear, 0)
    for i in range(send.shape[0]):
        send[i] = 0
    for k in range(plan.shape[0]):
        for j in range(3):
            plan[k, j] = 0
        plan[k, 3] = -1

    def first_choice(h, _):
        for k in range(TASKS):
            s1, s2 = table[h, RECORDS + 4 * k + 1], table[h, RECORDS + 4 * k + 2]
            b1, b2 = table[s1, FACTOR_ROUTE + h], table[s2, FACTOR_ROUTE + h]
            n1, n2 = uses[s1 * FPG + b1], uses[s2 * FPG + b2]
            at_first = 2 * load[s1] - jnp.where(n2 > 0, 0, FAST - sent[s2])
            at_second = 2 * load[s2] - jnp.where(n1 > 0, 0, FAST - sent[s1])
            second = (at_first > at_second) & (s1 != s2)
            c, o = jnp.where(second, s2, s1), jnp.where(second, s1, s2)
            y, x = jnp.where(second, b2, b1), jnp.where(second, b1, b2)
            n = jnp.where(second, n1, n2)
            moved = jnp.where(c != o, 1, 0)
            i = h * TASKS + k
            compute[i], other[i], compute_block[i], other_block[i] = c, o, y, x
            load[c] += 1
            sent[o] += jnp.where(n == 0, moved, 0)
            uses[o * FPG + x] = n + moved
        return 0

    lax.fori_loop(0, groups, first_choice, 0)
    over = lambda n: jnp.maximum(n - FAST, 0)

    def excess():
        total = 0
        for g in range(groups):
            total += over(load[g]) + over(sent[g])
        return total

    def sweep(state):
        def visit(i, bad):
            c, o = compute[i], other[i]
            wanted = (c != o) & ((load[c] > FAST) | (sent[o] > FAST))

            def flip(bad):
                y, x = compute_block[i], other_block[i]
                nc, no = uses[c * FPG + y], uses[o * FPG + x]
                less, more = jnp.where(no == 1, 1, 0), jnp.where(nc == 0, 1, 0)
                lc, lo, sc, so = load[c], load[o], sent[c], sent[o]
                change = over(lc - 1) - over(lc) + over(lo + 1) - over(lo)
                change += over(sc + more) - over(sc) + over(so - less) - over(so)

                def take(bad):
                    compute[i], other[i], compute_block[i], other_block[i] = o, c, x, y
                    load[c], load[o] = lc - 1, lo + 1
                    sent[c], sent[o] = sc + more, so - less
                    uses[c * FPG + y], uses[o * FPG + x] = nc + 1, no - 1
                    return bad + change

                return lax.cond(change <= 0, take, lambda bad: bad, bad)

            return lax.cond(wanted, flip, lambda bad: bad, bad)

        return state[0] + 1, lax.fori_loop(0, groups * TASKS, visit, state[1])

    _, bad = lax.while_loop(lambda s: (s[0] < SWEEPS) & (s[1] > 0), sweep, (jnp.int32(0), excess()))
    good = bad == 0
    balanced[0] = jnp.where(good, 1, 0)
    stride = jnp.where(good, FAST, FPG)

    def fetch(source, block, c):
        remote = source != c
        known = where_sent[source * FPG + block]
        fresh = remote & (known < 0)
        count = filled[source]
        at = jnp.where(fresh, count, known)
        filled[source] = count + jnp.where(fresh, 1, 0)
        where_sent[source * FPG + block] = at
        send[jnp.where(fresh & (source == mine), at, FPG)] = block
        slot = slots[c]
        slots[c] = slot + jnp.where(remote, 1, 0)
        pick[jnp.where(remote, c * FPG + slot, groups * FPG)] = source * stride + at
        return jnp.where(remote, FPG + slot, block)

    def note(h, k, c, left, right):
        o, s3 = table[h, RECORDS + 4 * k], table[h, RECORDS + 4 * k + 3]
        t = load[c]
        load[c] = t + 1
        row = jnp.where(c == mine, t, FAST)
        plan[row, 0] = left
        plan[row, 1] = right
        plan[row, 2] = s3 * (APG + 1) + table[s3, h]
        plan[row, 3] = o * TPG + table[o, TARGET + h]

    def deal_balanced(h, _):
        for k in range(TASKS):
            i = h * TASKS + k
            c, y = compute[i], compute_block[i]
            found = fetch(other[i], other_block[i], c)
            first = c == table[h, RECORDS + 4 * k + 1]
            note(h, k, c, jnp.where(first, y, found), jnp.where(first, found, y))
        return 0

    def deal_at_helper(h, _):
        for k in range(TASKS):
            s1, s2 = table[h, RECORDS + 4 * k + 1], table[h, RECORDS + 4 * k + 2]
            left = fetch(s1, table[s1, FACTOR_ROUTE + h], h)
            right = fetch(s2, table[s2, FACTOR_ROUTE + h], h)
            note(h, k, h, left, right)
        return 0

    for g in range(groups):
        load[g] = 0

    @pl.when(good)
    def _():
        lax.fori_loop(0, groups, deal_balanced, 0)

    @pl.when(jnp.logical_not(good))
    def _():
        lax.fori_loop(0, groups, deal_at_helper, 0)


def assign(me, table):
    groups = table.shape[0]
    smem = pl.BlockSpec(memory_space=pltpu.SMEM)
    one = lambda n: pltpu.SMEM((n,), jnp.int32)
    tasks = groups * TASKS
    return pl.pallas_call(
        assign_kernel,
        in_specs=[smem, smem],
        out_specs=[smem] * 4,
        out_shape=[
            jax.ShapeDtypeStruct((2 * FPG,), jnp.int32),
            jax.ShapeDtypeStruct(((groups + 1) * FPG,), jnp.int32),
            jax.ShapeDtypeStruct((2 * FAST, 4), jnp.int32),
            jax.ShapeDtypeStruct((1,), jnp.int32),
        ],
        scratch_shapes=[one(tasks)] * 4 + [one(groups)] * 2 + [one(groups * FPG)] + [one(groups)] * 2 + [one(groups * FPG)],
        name="assign",
    )(me, table)


def leave_kernel(send, factors, out, held, arrive):
    pieces, count, rows, _ = out.shape
    width = factors.shape[2]
    blocks = [pltpu.make_async_copy(factors.at[send[i]], held.at[i], arrive.at[i]) for i in range(count)]
    for block in blocks:
        block.start()
    for i, block in enumerate(blocks):
        block.wait()
        for piece in range(pieces):
            half, part = divmod(piece, width // LANES)
            out[piece, i] = held[i, half * rows : (half + 1) * rows, part * LANES : (part + 1) * LANES]


def leaving_pieces(send, factors, count, pieces):
    _, rows, width = factors.shape
    piece_rows = rows * width // LANES // pieces
    return pl.pallas_call(
        leave_kernel,
        in_specs=[pl.BlockSpec(memory_space=pltpu.SMEM), pl.BlockSpec(memory_space=pl.ANY)],
        out_specs=pl.BlockSpec(memory_space=pltpu.VMEM),
        out_shape=jax.ShapeDtypeStruct((pieces, count, piece_rows, LANES), factors.dtype),
        scratch_shapes=[
            pltpu.VMEM((count, rows, width), factors.dtype),
            pltpu.SemaphoreType.DMA((count,)),
        ],
        compiler_params=pltpu.CompilerParams(vmem_limit_bytes=16 << 20),
        name="leaving_pieces",
    )(send, factors)


def deal_kernel(pick, pieces, out):
    for g in range(out.shape[0]):
        for j in range(out.shape[1]):
            out[g, j] = pieces[pick[g * FPG + j]]


def dealt_pieces(pick, pieces, groups, slots):
    count, rows, lanes = pieces.shape
    return pl.pallas_call(
        deal_kernel,
        in_specs=[pl.BlockSpec(memory_space=pltpu.SMEM), pl.BlockSpec(memory_space=pltpu.VMEM)],
        out_specs=pl.BlockSpec(memory_space=pltpu.VMEM),
        out_shape=jax.ShapeDtypeStruct((groups, slots, rows, lanes), pieces.dtype),
        compiler_params=pltpu.CompilerParams(vmem_limit_bytes=12 << 20),
        name="dealt_pieces",
    )(pick, pieces)


def spread(held, axis, bits):
    members = lax.axis_size(axis)
    me = lax.axis_index(axis)
    for bit in bits:
        other = lax.ppermute(held, axis, [(i, i ^ bit) for i in range(members)])
        mine_first = (me & bit) == 0
        held = jnp.where(
            mine_first, jnp.concatenate([held, other]), jnp.concatenate([other, held])
        )
    return held


def facts_kernel(shard, amplitudes, amp_route, factor_route, target_tile, task_list, out):
    tiles, occupied, width = amplitudes.shape
    chosen = lax.broadcasted_iota(jnp.int32, (occupied, width), 0) == shard[0]
    facts = [amp_route[...], factor_route[...], target_tile[...]]
    facts += [task_list[k] for k in range(TASKS)]
    facts = jnp.concatenate(facts, axis=1).astype(jnp.float32)
    facts = jnp.concatenate([facts, jnp.zeros((1, LANES - facts.shape[1]), jnp.float32)], axis=1)
    parts = width // LANES
    for i in range(tiles + 1):
        if i < tiles:
            row = jnp.sum(jnp.where(chosen, amplitudes[i].astype(jnp.float32), 0.0), axis=0, keepdims=True)
            rows = [row[:, c * LANES : (c + 1) * LANES] for c in range(parts)]
        else:
            rows = [facts] + [jnp.zeros_like(facts)] * (parts - 1)
        tile = jnp.concatenate(rows, axis=0).astype(out.dtype)
        for g in range(out.shape[0]):
            out[g, i] = tile


def group_facts(amplitudes, factor_route, amp_route, task_list, target_tile):
    groups = lax.axis_size("group")
    tiles, _, width = amplitudes.shape
    shard = lax.axis_index("shard").astype(jnp.int32).reshape(1)
    vmem = pl.BlockSpec(memory_space=pltpu.VMEM)
    facts = pl.pallas_call(
        facts_kernel,
        in_specs=[pl.BlockSpec(memory_space=pltpu.SMEM)] + [vmem] * 5,
        out_specs=vmem,
        out_shape=jax.ShapeDtypeStruct((groups, tiles + 1, width // LANES, LANES), amplitudes.dtype),
        name="facts",
    )(shard, amplitudes, amp_route, factor_route, target_tile, task_list.transpose(1, 0, 2))
    held = lax.all_to_all(facts, "group", split_axis=0, concat_axis=0, tiled=True)
    return held.reshape(groups * (tiles + 1), *held.shape[2:]), held[:, tiles, 0].astype(jnp.int32)


def contributions(blocks_sent, slots, factors, amp_rows, send, pick, plan):
    groups = lax.axis_size("group")
    width = factors.shape[2]
    leaving = leaving_pieces(send, factors, blocks_sent, groups)
    held = lax.all_to_all(leaving, "group", split_axis=0, concat_axis=0, tiled=True)
    chosen = amp_rows.at[plan[:FAST, 2]].get(mode="promise_in_bounds")
    amps = spread(chosen[None], "shard", (1, 2, 4))
    held, amps = lax.optimization_barrier((held, amps))
    dealt = dealt_pieces(pick, held.reshape(groups * blocks_sent, *held.shape[2:]), groups, slots)
    arrived = lax.all_to_all(dealt, "group", split_axis=0, concat_axis=0, tiled=True)
    amps = spread(amps, "shard", (8, 16))
    amps = amps.reshape(-1, FAST, width).transpose(1, 0, 2)
    return ladder(plan, factors, arrived, amps)


def body(factors, amplitudes, factor_route, amp_route, task_list, target_tile):
    groups = lax.axis_size("group")
    amp_rows, table = group_facts(amplitudes, factor_route, amp_route, task_list, target_tile)
    me = lax.axis_index("group").astype(jnp.int32).reshape(1)
    send, pick, plan, balanced = assign(me, table)
    operands = (factors, amp_rows, send, pick, plan)
    parts = lax.cond(
        balanced[0] == 1,
        functools.partial(contributions, FAST, FAST),
        functools.partial(contributions, FPG, 2 * TASKS),
        *operands,
    )
    pieces = lax.all_to_all(parts, "shard", split_axis=0, concat_axis=0, tiled=True)
    returns = combine(plan, pieces, groups * TPG)
    arrived = lax.all_to_all(returns, "group", split_axis=0, concat_axis=0, tiled=True)
    return owned(arrived.reshape(groups, TPG, *arrived.shape[1:]))


def solution(mesh):
    return jax.shard_map(
        body,
        mesh=mesh,
        in_specs=(
            P("group", "shard", None),
            P("group", None, None),
            P("group", None),
            P("group", None),
            P("group", None, None),
            P("group", None),
        ),
        out_specs=P("group", None, "shard"),
        check_vma=False,
    )
```

```python
import functools

import jax
import jax.numpy as jnp
from jax import lax
from jax.experimental import pallas as pl
from jax.experimental.pallas import tpu as pltpu
from jax.sharding import PartitionSpec as P

VB = 32
FPG = 8
APG = 4
TPG = 2
TASKS = 3
LANES = 128
FAST = 4
SWEEPS = 12
FACTOR_ROUTE, TARGET, RECORDS = 16, 32, 48
FOLD = LANES // VB


def swap_lane_blocks(tiles, unit):
    lane = lax.broadcasted_iota(jnp.int32, tiles[0].shape, 1)
    low = (lane % (4 * unit)).astype(tiles[0].dtype) < 2 * unit
    even = (lane % (2 * unit)).astype(tiles[0].dtype) < unit
    x0, x1, x2, x3 = tiles
    y0 = jnp.where(low, x0, pltpu.roll(x2, 2 * unit, 1))
    y2 = jnp.where(low, pltpu.roll(x0, LANES - 2 * unit, 1), x2)
    y1 = jnp.where(low, x1, pltpu.roll(x3, 2 * unit, 1))
    y3 = jnp.where(low, pltpu.roll(x1, LANES - 2 * unit, 1), x3)
    z0 = jnp.where(even, y0, pltpu.roll(y1, unit, 1))
    z1 = jnp.where(even, pltpu.roll(y0, LANES - unit, 1), y1)
    z2 = jnp.where(even, y2, pltpu.roll(y3, unit, 1))
    z3 = jnp.where(even, pltpu.roll(y2, LANES - unit, 1), y3)
    return z0, z1, z2, z3


def swap_pairs(source, swap, out):
    count, width = source.shape
    span = swap.shape[0]
    for group in range(width // span):
        columns = slice(group * span, (group + 1) * span)
        out[:, columns] = jnp.dot(source[:, columns], swap[...], preferred_element_type=jnp.float32).astype(out.dtype)
    for chunk in range(count // VB):
        rows = slice(chunk * VB, (chunk + 1) * VB)
        for odd in range(2):
            lanes = [slice((2 * i + odd) * LANES, (2 * i + odd + 1) * LANES) for i in range(FOLD)]
            tiles = swap_lane_blocks([out[rows, at] for at in lanes], VB // FOLD)
            for at, tile in zip(lanes, tiles):
                out[rows, at] = tile


def assemble(select, whole, cut, out):
    @pl.when(select < FPG)
    def _():
        out[...] = whole[0]

    @pl.when(select >= FPG)
    def _():
        rows = cut.shape[2]
        for piece in range(cut.shape[0]):
            half, part = divmod(piece, out.shape[1] // LANES)
            out[half * rows : (half + 1) * rows, part * LANES : (part + 1) * LANES] = cut[piece, 0]


def ladder_kernel(
    plan, left_whole, left_cut, right_whole, right_cut, amp, swap, out,
    left, right, right_t, amp_t, integral, folded, result,
):
    task = pl.program_id(0)

    @pl.when(plan[task, 3] < 0)
    def _():
        out[...] = jnp.zeros_like(out)

    @pl.when(plan[task, 3] >= 0)
    def _():
        assemble(plan[task, 0], left_whole, left_cut, left)
        assemble(plan[task, 1], right_whole, right_cut, right)
        ladder_task(left, right, amp, swap, out, right_t, amp_t, integral, folded, result)


def ladder_task(left, right, amp, swap, out, right_t, amp_t, integral, folded, result):
    width = left.shape[1]
    occupied = amp.shape[1]
    per_pass = 2 * FOLD
    span = per_pass * VB
    swap_pairs(right, swap, right_t)
    swap_pairs(amp.at[0], swap, amp_t)

    def products(step, _):
        columns = pl.ds(pl.multiple_of(step * 2 * span, 2 * span), 2 * span)
        integral[columns, :] = lax.dot_general(
            left[:, columns], right_t[...], (((0,), (0,)), ((), ())), preferred_element_type=jnp.float32
        ).astype(jnp.bfloat16)
        return 0

    lax.fori_loop(0, VB // per_pass // 2, products, 0)

    def one_pass(step, _):
        columns = pl.ds(pl.multiple_of(step * span, span), span)
        for part in range(width // LANES):
            lanes = slice(part * LANES, (part + 1) * LANES)
            for half in range(2):
                rows = half * FOLD * VB
                tiles = [
                    integral[pl.ds(pl.multiple_of(step * span + rows + a * VB, VB), VB), lanes] for a in range(FOLD)
                ]
                for d, tile in enumerate(swap_lane_blocks(tiles, VB)):
                    base = (part * FOLD + d) * VB
                    folded[base : base + VB, half * LANES : (half + 1) * LANES] = tile
        result[:, columns] = jnp.dot(amp_t[...], folded[...], preferred_element_type=jnp.float32)
        return 0

    lax.fori_loop(0, VB // per_pass, one_pass, 0)
    band = occupied // FOLD
    for group in range(width // LANES):
        lanes = slice(group * LANES, (group + 1) * LANES)
        tiles = [result[i * band : (i + 1) * band, lanes] for i in range(FOLD)]
        for a, tile in enumerate(swap_lane_blocks(tiles, VB)):
            out[group * FOLD + a, 0] = tile.astype(out.dtype)


def ladder(plan, factors, arrived, amps):
    rows, width = factors.shape[1:]
    tasks, occupied = amps.shape[:2]
    span = 2 * LANES
    index = jnp.arange(span, dtype=jnp.int32)
    p, q = index // VB, index % VB
    swap = ((q % 8 * VB + q // 8 * 8 + p)[:, None] == index[None, :]).astype(jnp.bfloat16)
    band = occupied // FOLD
    pieces, _, piece_rows, _ = arrived.shape

    def whole(side):
        def place(k, plan):
            return jnp.where(plan[k, side] < FPG, plan[k, side], 0), 0, 0

        return pl.BlockSpec((1, rows, width), place)

    def cut(side):
        def place(k, plan):
            return 0, jnp.where(plan[k, side] < FPG, 0, plan[k, side] - FPG), 0, 0

        return pl.BlockSpec((pieces, 1, piece_rows, LANES), place)

    return pl.pallas_call(
        ladder_kernel,
        grid_spec=pltpu.PrefetchScalarGridSpec(
            num_scalar_prefetch=1,
            grid=(tasks,),
            in_specs=[
                whole(0),
                cut(0),
                whole(1),
                cut(1),
                pl.BlockSpec((1, occupied, width), lambda k, plan: (k, 0, 0)),
                pl.BlockSpec((span, span), lambda k, plan: (0, 0)),
            ],
            out_specs=pl.BlockSpec((VB, 1, band, LANES), lambda k, plan: (0, k, 0, 0)),
            scratch_shapes=[
                pltpu.VMEM((rows, width), jnp.bfloat16),
                pltpu.VMEM((rows, width), jnp.bfloat16),
                pltpu.VMEM((rows, width), jnp.bfloat16),
                pltpu.VMEM((occupied, width), jnp.bfloat16),
                pltpu.VMEM((width, width), jnp.bfloat16),
                pltpu.VMEM((width, 2 * LANES), jnp.bfloat16),
                pltpu.VMEM((occupied, width), jnp.float32),
            ],
        ),
        out_shape=jax.ShapeDtypeStruct((VB, tasks, band, LANES), jnp.bfloat16),
        compiler_params=pltpu.CompilerParams(dimension_semantics=("arbitrary",)),
        name="ladder",
    )(plan, factors, arrived, factors, arrived, amps, swap)


def combine_kernel(plan, pieces, out):
    total = jnp.sum(pieces[...].astype(jnp.float32), axis=0)
    out[...] = jnp.zeros_like(out)
    for k in range(pieces.shape[1]):
        target = plan[k, 3]

        @pl.when(target >= 0)
        def _():
            out[target] += total[k]


def combine(plan, pieces, tiles):
    return pl.pallas_call(
        combine_kernel,
        in_specs=[pl.BlockSpec(memory_space=pltpu.SMEM), pl.BlockSpec(memory_space=pltpu.VMEM)],
        out_specs=pl.BlockSpec(memory_space=pltpu.VMEM),
        out_shape=jax.ShapeDtypeStruct((tiles, *pieces.shape[2:]), jnp.float32),
        name="combine",
    )(plan, pieces)


def owned_kernel(arrived, out):
    groups, tiles, band, lanes = arrived.shape
    for t in range(tiles):
        total = jnp.sum(arrived[:, t], axis=0)
        for i in range(FOLD):
            out[t, i * band : (i + 1) * band, :] = total[:, i * VB : (i + 1) * VB]


def owned(arrived):
    groups, tiles, band, lanes = arrived.shape
    return pl.pallas_call(
        owned_kernel,
        in_specs=[pl.BlockSpec(memory_space=pltpu.VMEM)],
        out_specs=pl.BlockSpec(memory_space=pltpu.VMEM),
        out_shape=jax.ShapeDtypeStruct((tiles, band * FOLD, VB), jnp.float32),
        name="owned",
    )(arrived)


def assign_kernel(
    me, table, factors, send, pick, plan, balanced, ready,
    compute, other, compute_block, other_block, load, sent, uses, filled, slots, where_sent,
):
    groups = table.shape[0]
    mine = me[0]
    for g in range(groups):
        load[g] = 0
        sent[g] = 0
        filled[g] = 0
        slots[g] = 0

    def clear(i, _):
        for j in range(FPG):
            uses[i * FPG + j] = 0
            where_sent[i * FPG + j] = -1
            pick[i * FPG + j] = 0
        return 0

    lax.fori_loop(0, groups, clear, 0)
    for i in range(send.shape[0]):
        send[i] = 0
    for k in range(plan.shape[0]):
        for j in range(3):
            plan[k, j] = 0
        plan[k, 3] = -1

    def first_choice(h, _):
        for k in range(TASKS):
            s1, s2 = table[h, RECORDS + 4 * k + 1], table[h, RECORDS + 4 * k + 2]
            b1, b2 = table[s1, FACTOR_ROUTE + h], table[s2, FACTOR_ROUTE + h]
            n1, n2 = uses[s1 * FPG + b1], uses[s2 * FPG + b2]
            at_first = 2 * load[s1] - jnp.where(n2 > 0, 0, FAST - sent[s2])
            at_second = 2 * load[s2] - jnp.where(n1 > 0, 0, FAST - sent[s1])
            second = (at_first > at_second) & (s1 != s2)
            c, o = jnp.where(second, s2, s1), jnp.where(second, s1, s2)
            y, x = jnp.where(second, b2, b1), jnp.where(second, b1, b2)
            n = jnp.where(second, n1, n2)
            moved = jnp.where(c != o, 1, 0)
            i = h * TASKS + k
            compute[i], other[i], compute_block[i], other_block[i] = c, o, y, x
            load[c] += 1
            sent[o] += jnp.where(n == 0, moved, 0)
            uses[o * FPG + x] = n + moved
        return 0

    lax.fori_loop(0, groups, first_choice, 0)
    over = lambda n: jnp.maximum(n - FAST, 0)

    def excess():
        total = 0
        for g in range(groups):
            total += over(load[g]) + over(sent[g])
        return total

    def sweep(state):
        def visit(i, bad):
            c, o = compute[i], other[i]
            wanted = (c != o) & ((load[c] > FAST) | (sent[o] > FAST))

            def flip(bad):
                y, x = compute_block[i], other_block[i]
                nc, no = uses[c * FPG + y], uses[o * FPG + x]
                less, more = jnp.where(no == 1, 1, 0), jnp.where(nc == 0, 1, 0)
                lc, lo, sc, so = load[c], load[o], sent[c], sent[o]
                change = over(lc - 1) - over(lc) + over(lo + 1) - over(lo)
                change += over(sc + more) - over(sc) + over(so - less) - over(so)

                def take(bad):
                    compute[i], other[i], compute_block[i], other_block[i] = o, c, x, y
                    load[c], load[o] = lc - 1, lo + 1
                    sent[c], sent[o] = sc + more, so - less
                    uses[c * FPG + y], uses[o * FPG + x] = nc + 1, no - 1
                    return bad + change

                return lax.cond(change <= 0, take, lambda bad: bad, bad)

            return lax.cond(wanted, flip, lambda bad: bad, bad)

        return state[0] + 1, lax.fori_loop(0, groups * TASKS, visit, state[1])

    _, bad = lax.while_loop(lambda s: (s[0] < SWEEPS) & (s[1] > 0), sweep, (jnp.int32(0), excess()))
    good = bad == 0
    balanced[0] = jnp.where(good, 1, 0)
    stride = jnp.where(good, FAST, FPG)

    def fetch(source, block, c):
        remote = source != c
        known = where_sent[source * FPG + block]
        fresh = remote & (known < 0)
        count = filled[source]
        at = jnp.where(fresh, count, known)
        filled[source] = count + jnp.where(fresh, 1, 0)
        where_sent[source * FPG + block] = at
        send[jnp.where(fresh & (source == mine), at, FPG)] = block
        slot = slots[c]
        slots[c] = slot + jnp.where(remote, 1, 0)
        pick[jnp.where(remote, c * FPG + slot, groups * FPG)] = source * stride + at
        return jnp.where(remote, FPG + slot, block)

    def note(h, k, c, left, right):
        o, s3 = table[h, RECORDS + 4 * k], table[h, RECORDS + 4 * k + 3]
        t = load[c]
        load[c] = t + 1
        row = jnp.where(c == mine, t, FAST)
        plan[row, 0] = left
        plan[row, 1] = right
        plan[row, 2] = s3 * (APG + 1) + table[s3, h]
        plan[row, 3] = o * TPG + table[o, TARGET + h]

    def deal_balanced(h, _):
        for k in range(TASKS):
            i = h * TASKS + k
            c, y = compute[i], compute_block[i]
            found = fetch(other[i], other_block[i], c)
            first = c == table[h, RECORDS + 4 * k + 1]
            note(h, k, c, jnp.where(first, y, found), jnp.where(first, found, y))
        return 0

    def deal_at_helper(h, _):
        for k in range(TASKS):
            s1, s2 = table[h, RECORDS + 4 * k + 1], table[h, RECORDS + 4 * k + 2]
            left = fetch(s1, table[s1, FACTOR_ROUTE + h], h)
            right = fetch(s2, table[s2, FACTOR_ROUTE + h], h)
            note(h, k, h, left, right)
        return 0

    for g in range(groups):
        load[g] = 0

    @pl.when(good)
    def _():
        lax.fori_loop(0, groups, deal_balanced, 0)

    @pl.when(jnp.logical_not(good))
    def _():
        lax.fori_loop(0, groups, deal_at_helper, 0)

    pieces, count, rows, _ = ready.shape
    for i in range(count):
        for piece in range(pieces):
            half, part = divmod(piece, factors.shape[2] // LANES)
            ready[piece, i] = factors[send[i], half * rows : (half + 1) * rows, part * LANES : (part + 1) * LANES]


def assign(me, table, factors):
    groups = table.shape[0]
    smem, vmem = pl.BlockSpec(memory_space=pltpu.SMEM), pl.BlockSpec(memory_space=pltpu.VMEM)
    _, rows, width = factors.shape
    one = lambda n: pltpu.SMEM((n,), jnp.int32)
    tasks = groups * TASKS
    return pl.pallas_call(
        assign_kernel,
        in_specs=[smem, smem, vmem],
        out_specs=[smem] * 4 + [vmem],
        out_shape=[
            jax.ShapeDtypeStruct((2 * FPG,), jnp.int32),
            jax.ShapeDtypeStruct(((groups + 1) * FPG,), jnp.int32),
            jax.ShapeDtypeStruct((2 * FAST, 4), jnp.int32),
            jax.ShapeDtypeStruct((1,), jnp.int32),
            jax.ShapeDtypeStruct((groups, FAST, rows * width // LANES // groups, LANES), factors.dtype),
        ],
        scratch_shapes=[one(tasks)] * 4 + [one(groups)] * 2 + [one(groups * FPG)] + [one(groups)] * 2 + [one(groups * FPG)],
        compiler_params=pltpu.CompilerParams(vmem_limit_bytes=12 << 20),
        name="assign",
    )(me, table, factors)


def leave_kernel(send, factors, out, held, arrive):
    pieces, count, rows, _ = out.shape
    width = factors.shape[2]
    blocks = [pltpu.make_async_copy(factors.at[send[i]], held.at[i], arrive.at[i]) for i in range(count)]
    for block in blocks:
        block.start()
    for i, block in enumerate(blocks):
        block.wait()
        for piece in range(pieces):
            half, part = divmod(piece, width // LANES)
            out[piece, i] = held[i, half * rows : (half + 1) * rows, part * LANES : (part + 1) * LANES]


def leaving_pieces(send, factors, count, pieces):
    _, rows, width = factors.shape
    piece_rows = rows * width // LANES // pieces
    return pl.pallas_call(
        leave_kernel,
        in_specs=[pl.BlockSpec(memory_space=pltpu.SMEM), pl.BlockSpec(memory_space=pl.ANY)],
        out_specs=pl.BlockSpec(memory_space=pltpu.VMEM),
        out_shape=jax.ShapeDtypeStruct((pieces, count, piece_rows, LANES), factors.dtype),
        scratch_shapes=[
            pltpu.VMEM((count, rows, width), factors.dtype),
            pltpu.SemaphoreType.DMA((count,)),
        ],
        compiler_params=pltpu.CompilerParams(vmem_limit_bytes=16 << 20),
        name="leaving_pieces",
    )(send, factors)


def deal_kernel(pick, pieces, out):
    for g in range(out.shape[0]):
        for j in range(out.shape[1]):
            out[g, j] = pieces[pick[g * FPG + j]]


def dealt_pieces(pick, pieces, groups, slots):
    count, rows, lanes = pieces.shape
    return pl.pallas_call(
        deal_kernel,
        in_specs=[pl.BlockSpec(memory_space=pltpu.SMEM), pl.BlockSpec(memory_space=pltpu.VMEM)],
        out_specs=pl.BlockSpec(memory_space=pltpu.VMEM),
        out_shape=jax.ShapeDtypeStruct((groups, slots, rows, lanes), pieces.dtype),
        compiler_params=pltpu.CompilerParams(vmem_limit_bytes=12 << 20),
        name="dealt_pieces",
    )(pick, pieces)


def spread(held, axis, bits):
    members = lax.axis_size(axis)
    me = lax.axis_index(axis)
    for bit in bits:
        other = lax.ppermute(held, axis, [(i, i ^ bit) for i in range(members)])
        mine_first = (me & bit) == 0
        held = jnp.where(
            mine_first, jnp.concatenate([held, other]), jnp.concatenate([other, held])
        )
    return held


def facts_kernel(shard, amplitudes, amp_route, factor_route, target_tile, task_list, out):
    tiles, occupied, width = amplitudes.shape
    chosen = lax.broadcasted_iota(jnp.int32, (occupied, width), 0) == shard[0]
    facts = [amp_route[...], factor_route[...], target_tile[...]]
    facts += [task_list[k] for k in range(TASKS)]
    facts = jnp.concatenate(facts, axis=1).astype(jnp.float32)
    facts = jnp.concatenate([facts, jnp.zeros((1, LANES - facts.shape[1]), jnp.float32)], axis=1)
    parts = width // LANES
    for i in range(tiles + 1):
        if i < tiles:
            row = jnp.sum(jnp.where(chosen, amplitudes[i].astype(jnp.float32), 0.0), axis=0, keepdims=True)
            rows = [row[:, c * LANES : (c + 1) * LANES] for c in range(parts)]
        else:
            rows = [facts] + [jnp.zeros_like(facts)] * (parts - 1)
        tile = jnp.concatenate(rows, axis=0).astype(out.dtype)
        for g in range(out.shape[0]):
            out[g, i] = tile


def group_facts(amplitudes, factor_route, amp_route, task_list, target_tile):
    groups = lax.axis_size("group")
    tiles, _, width = amplitudes.shape
    shard = lax.axis_index("shard").astype(jnp.int32).reshape(1)
    vmem = pl.BlockSpec(memory_space=pltpu.VMEM)
    facts = pl.pallas_call(
        facts_kernel,
        in_specs=[pl.BlockSpec(memory_space=pltpu.SMEM)] + [vmem] * 5,
        out_specs=vmem,
        out_shape=jax.ShapeDtypeStruct((groups, tiles + 1, width // LANES, LANES), amplitudes.dtype),
        name="facts",
    )(shard, amplitudes, amp_route, factor_route, target_tile, task_list.transpose(1, 0, 2))
    held = lax.all_to_all(facts, "group", split_axis=0, concat_axis=0, tiled=True)
    return held.reshape(groups * (tiles + 1), *held.shape[2:]), held[:, tiles, 0].astype(jnp.int32)


def contributions(blocks_sent, slots, factors, ready, amp_rows, send, pick, plan):
    groups = lax.axis_size("group")
    width = factors.shape[2]
    leaving = ready
    if blocks_sent > FAST:
        leaving = leaving_pieces(send, factors, blocks_sent, groups)
    held = lax.all_to_all(leaving, "group", split_axis=0, concat_axis=0, tiled=True)
    chosen = amp_rows.at[plan[:FAST, 2]].get(mode="promise_in_bounds")
    amps = spread(chosen[None], "shard", (1, 2, 4))
    held, amps = lax.optimization_barrier((held, amps))
    dealt = dealt_pieces(pick, held.reshape(groups * blocks_sent, *held.shape[2:]), groups, slots)
    arrived = lax.all_to_all(dealt, "group", split_axis=0, concat_axis=0, tiled=True)
    amps = spread(amps, "shard", (8, 16))
    amps = amps.reshape(-1, FAST, width).transpose(1, 0, 2)
    return ladder(plan, factors, arrived, amps)


def body(factors, amplitudes, factor_route, amp_route, task_list, target_tile):
    groups = lax.axis_size("group")
    amp_rows, table = group_facts(amplitudes, factor_route, amp_route, task_list, target_tile)
    me = lax.axis_index("group").astype(jnp.int32).reshape(1)
    send, pick, plan, balanced, ready = assign(me, table, factors)
    operands = (factors, ready, amp_rows, send, pick, plan)
    parts = lax.cond(
        balanced[0] == 1,
        functools.partial(contributions, FAST, FAST),
        functools.partial(contributions, FPG, 2 * TASKS),
        *operands,
    )
    pieces = lax.all_to_all(parts, "shard", split_axis=0, concat_axis=0, tiled=True)
    returns = combine(plan, pieces, groups * TPG)
    arrived = lax.all_to_all(returns, "group", split_axis=0, concat_axis=0, tiled=True)
    return owned(arrived.reshape(groups, TPG, *arrived.shape[1:]))


def solution(mesh):
    return jax.shard_map(
        body,
        mesh=mesh,
        in_specs=(
            P("group", "shard", None),
            P("group", None, None),
            P("group", None),
            P("group", None),
            P("group", None, None),
            P("group", None),
        ),
        out_specs=P("group", None, "shard"),
        check_vma=False,
    )
```
